32 devices in a mesh: groups: 1, dp: 16 (over z, y, x), tp: 2 (over core).
Axes of the slice: x: 2, y: 2, z: 4, core: 2. Of those that a mesh axis runs over, the one named last changes fastest.
Arguments:
- pool: bfloat16 [2048, 4608], P(('groups', 'dp')), may hold values from -10 to 10
- page_holder: int32 [896], P(('groups', 'dp')), may hold values from 0 to 15, as said below
- page_slot: int32 [896], P(('groups', 'dp')), may hold values from 0 to 127
- suffix_latent_rows: bfloat16 [16, 9216], P(('groups', 'dp')), may hold values from -5 to 5
- prefill_queries: bfloat16 [16, 128, 4608], P(('groups', 'dp'), None, 'tp'), may hold values from -10 to 10
- suffix_len: int32 [2], P('groups'), may hold values from 1 to 128
- decode_queries: bfloat16 [64, 36864], P(('groups', 'dp'), 'tp'), may hold values from -10 to 10
- decode_len: int32 [64], P(('groups', 'dp')), may hold values from 1 to 256
Outputs:
- prefill_output: bfloat16 [16, 128, 4096], P(('groups', 'dp'), None, 'tp')
- decode_out: bfloat16 [64, 32768], P(('groups', 'dp'), 'tp')
The draws below stay inside these ranges and needn't reach their ends.
Inputs may be any that keep to these rules, and one draw needn't show every extreme that they name: `page_holder`: within one device's 56 entries no holder appears more than 4 times, and some holder appears exactly 4 times.
All inputs are finite; a program needn't handle non-finite values.
Results may differ from the reference program's by a relative error of at most 0.004.
Values may be sent and summed in bfloat16 or wider, within the bound.
No kernel may reach another device: no remote copies, remote signals or barrier semaphores. Data moves between devices by JAX's collectives and lax.ppermute only.
A program may use at most 64 MiB of HBM per device.

```python
import jax
import jax.numpy as jnp
from jax import lax

ATTENTION_HEADS = 64
LATENT_WIDTH = 512
ROTARY_WIDTH = 64
PAGE_TOKENS = 8
SUFFIX_SHARE = 16
TEAM_RANKS = 8
PULL = 56
DECODE_ROWS_DP = 4
ROW_PAGES = 32
POOL_PAGES = 128
SUFFIX_TOKENS = 128
N_DP = 16


def query_block(key, leading, spread):
    compressed_width = LATENT_WIDTH + ROTARY_WIDTH
    drawn = jax.random.normal(jax.random.fold_in(key, 15), leading + (compressed_width,), jnp.float32) * spread
    return jnp.clip(drawn, -4.0 * spread, 4.0 * spread)


def draw_pool(key, part):
    row_count = N_DP * POOL_PAGES
    compressed_width = LATENT_WIDTH + ROTARY_WIDTH
    base_key = jax.random.fold_in(key, 4201)
    value_rows = jnp.clip(jax.random.normal(base_key, (row_count, PAGE_TOKENS, compressed_width), jnp.float32), -4.0, 4.0)
    return value_rows.reshape(row_count, PAGE_TOKENS * compressed_width).astype(jnp.bfloat16)


def draw_page_holder(key, part):
    subkeys = jax.random.split(jax.random.fold_in(key, 5303), N_DP)

    def draw_order(subkey):
        return jax.random.permutation(subkey, N_DP)
    orders = jax.vmap(draw_order)(subkeys)
    picks = jnp.arange(PULL, dtype=jnp.int32) % N_DP
    return orders[:, picks].reshape(N_DP * PULL).astype(jnp.int32)


def draw_prefill_queries(key, part):
    value_rows = query_block(jax.random.fold_in(key, 6101), (N_DP, SUFFIX_TOKENS, ATTENTION_HEADS // TEAM_RANKS), 1.4)
    return value_rows.reshape(N_DP, SUFFIX_TOKENS, ATTENTION_HEADS // TEAM_RANKS * (LATENT_WIDTH + ROTARY_WIDTH)).astype(jnp.bfloat16)


def draw_decode_queries(key, part):
    value_rows = query_block(jax.random.fold_in(key, 6202), (N_DP * DECODE_ROWS_DP, ATTENTION_HEADS), 1.0)
    return value_rows.reshape(N_DP * DECODE_ROWS_DP, ATTENTION_HEADS * (LATENT_WIDTH + ROTARY_WIDTH)).astype(jnp.bfloat16)


def place_ends(values, stream_key, least, high):
    place = [jax.random.randint(jax.random.fold_in(stream_key, axis), (), 0, length) for axis, length in enumerate(values.shape)]
    main_axis = values.shape.index(max(values.shape))
    beside = place[:main_axis] + [(place[main_axis] + 1) % values.shape[main_axis]] + place[main_axis + 1:]
    return values.at[tuple(place)].set(least).at[tuple(beside)].set(high)


def shard_levels(stream_key, shape, cuts, smallest, largest):
    level, own = 1.0, jax.random.fold_in(stream_key, 6)
    for axis_at, shards_of in cuts:
        steps = jnp.exp(jax.random.uniform(jax.random.fold_in(own, axis_at), (shards_of,), jnp.float32, smallest / len(cuts), largest / len(cuts)))
        level = level * jnp.repeat(steps, shape[axis_at] // shards_of).reshape([-1 if axis == axis_at else 1 for axis in range(len(shape))])
    return level


def noise(key, extent, deviation, limit, cuts=(), kind=jnp.bfloat16):
    entries = jax.random.normal(key, extent, jnp.float32) * deviation
    if len(cuts) > 0:
        entries = shard_levels(key, extent, cuts, -0.22, 0.18) * entries
    return jnp.clip(entries, min=-limit, max=limit).astype(kind)


def setup_inputs(seed: int = 0, part: int = 0) -> dict:
    key_list = jax.random.split(jax.random.key(seed), 9)
    part_keys = jax.random.split(jax.random.fold_in(key_list[8], part), 9)
    pool = draw_pool(jax.random.fold_in(jax.random.fold_in(key_list[8], part), 71), part)
    page_holder = draw_page_holder(jax.random.fold_in(jax.random.fold_in(key_list[8], part), 71), part)
    page_slot = place_ends(jax.random.randint(part_keys[2], (N_DP * PULL,), 0, POOL_PAGES), jax.random.fold_in(part_keys[2], 1), 0, POOL_PAGES - 1).astype(jnp.int32)
    suffix_latent_rows = noise(part_keys[3], (N_DP, SUFFIX_SHARE * (LATENT_WIDTH + ROTARY_WIDTH)), 1.25, 5.0, ((0, 16),))
    prefill_queries = draw_prefill_queries(jax.random.fold_in(jax.random.fold_in(key_list[8], part), 71), part)
    suffix_len = jax.random.randint(part_keys[5], (N_DP // TEAM_RANKS,), 1, SUFFIX_TOKENS + 1).astype(jnp.int32)
    decode_queries = draw_decode_queries(jax.random.fold_in(jax.random.fold_in(key_list[8], part), 71), part)
    decode_len = place_ends(jax.random.randint(part_keys[7], (N_DP * DECODE_ROWS_DP,), 1, ROW_PAGES * PAGE_TOKENS + 1), jax.random.fold_in(part_keys[7], 1), 1, ROW_PAGES * PAGE_TOKENS).astype(jnp.int32)
    return dict(pool=pool, page_holder=page_holder, page_slot=page_slot, suffix_latent_rows=suffix_latent_rows, prefill_queries=prefill_queries, suffix_len=suffix_len, decode_queries=decode_queries, decode_len=decode_len)


softmax_scale = 192.0 ** -0.5
masked_score = -1.0e30


def attend_rows(queries, key_matrix, allowed):
    scores = jnp.einsum('shr,kr->shk', queries.astype(jnp.float32), key_matrix.astype(jnp.float32)) * softmax_scale
    scores = jnp.where(allowed[:, None, :], scores, masked_score)
    row_peak = jnp.max(scores, axis=-1, keepdims=True)
    powers = jnp.exp(scores - row_peak)
    denominator = jnp.sum(powers, axis=-1)
    weights = powers.astype(jnp.bfloat16)
    value_rows = key_matrix[:, :LATENT_WIDTH]
    blended_output = jnp.einsum('shk,kc->shc', weights.astype(jnp.float32), value_rows.astype(jnp.float32))
    return blended_output / denominator[..., None]


def reference(pool, page_holder, page_slot, suffix_latent_rows, prefill_queries, suffix_len, decode_queries, decode_len):
    compressed_width = LATENT_WIDTH + ROTARY_WIDTH
    team_heads = ATTENTION_HEADS // TEAM_RANKS
    requests = N_DP // TEAM_RANKS
    holders = page_holder.reshape(requests, TEAM_RANKS * PULL)
    slot_table = page_slot.reshape(requests, TEAM_RANKS * PULL)
    suffixes = suffix_latent_rows.reshape(requests, SUFFIX_TOKENS, compressed_width)
    queries = prefill_queries.reshape(requests, TEAM_RANKS, SUFFIX_TOKENS, team_heads, compressed_width)
    positions = jnp.arange(SUFFIX_TOKENS, dtype=jnp.int32)
    prefix_count = TEAM_RANKS * PULL * PAGE_TOKENS

    def one_request(request_no):
        page_rows = pool[holders[request_no] * POOL_PAGES + slot_table[request_no]]
        key_matrix = jnp.concatenate([page_rows.reshape(prefix_count, compressed_width), suffixes[request_no]], axis=0)
        length = suffix_len[request_no]
        prefix_ok = jnp.ones((SUFFIX_TOKENS, prefix_count), dtype=bool)
        suffix_ok = (positions[None, :] <= positions[:, None]) & (positions[None, :] < length)
        allowed = jnp.concatenate([prefix_ok, suffix_ok], axis=1)

        def one_member(member_queries):
            return attend_rows(member_queries, key_matrix, allowed)

        blended_output = lax.map(one_member, queries[request_no])
        live_rows = positions < length
        blended_output = jnp.where(live_rows[None, :, None, None], blended_output, 0.0)
        return blended_output.reshape(TEAM_RANKS, SUFFIX_TOKENS, team_heads * LATENT_WIDTH).astype(jnp.bfloat16)

    prefill_output = lax.map(one_request, jnp.arange(requests, dtype=jnp.int32))
    prefill_output = prefill_output.reshape(N_DP, SUFFIX_TOKENS, team_heads * LATENT_WIDTH)

    contexts = pool.reshape(N_DP * DECODE_ROWS_DP, ROW_PAGES * PAGE_TOKENS, compressed_width)
    decode_rows = decode_queries.reshape(N_DP * DECODE_ROWS_DP, 1, ATTENTION_HEADS, compressed_width)
    key_positions = jnp.arange(ROW_PAGES * PAGE_TOKENS, dtype=jnp.int32)

    def one_row(items):
        row_queries, context_output, length = items
        allowed = (key_positions < length)[None, :]
        blended_output = attend_rows(row_queries, context_output, allowed)
        return blended_output.reshape(ATTENTION_HEADS * LATENT_WIDTH).astype(jnp.bfloat16)

    decode_out = lax.map(one_row, (decode_rows, contexts, decode_len))
    return prefill_output, decode_out
```

```python
import math

import jax
import jax.numpy as jnp
from jax import lax
from jax.experimental import pallas as pl
from jax.experimental.pallas import tpu as pltpu
from jax.sharding import PartitionSpec as P

LATENT_WIDTH = 512
ROTARY_WIDTH = 64
WIDTH = LATENT_WIDTH + ROTARY_WIDTH
PADDED = 640
PAIR = 2 * WIDTH
TEAM = 8
LANES = 128
SUFFIX_LANES = 384

softmax_scale = 192.0 ** (-0.5)
exp2_scale = softmax_scale * math.log2(math.e)
masked_score = -1e30


f32 = jnp.float32
bf16 = jnp.bfloat16


def iota(shape, dim):
    return lax.broadcasted_iota(jnp.int32, shape, dim)


def vmem():
    return pl.BlockSpec(memory_space=pltpu.VMEM)


def smem():
    return pl.BlockSpec(memory_space=pltpu.SMEM)


def call(body, n_smem, n_in, outs, **kw):
    return pl.pallas_call(
        body,
        in_specs=[smem()] * n_smem + [vmem()] * n_in,
        out_specs=tuple(vmem() for _ in outs) if len(outs) > 1 else vmem(),
        out_shape=tuple(outs) if len(outs) > 1 else outs[0],
        **kw,
    )


def xperm(value, masks):
    n, cores = lax.axis_size("dp"), lax.axis_size("tp")
    pairs = [(d * cores + c, (d ^ masks[c % 2]) * cores + c) for d in range(n) for c in range(cores)]
    return lax.ppermute(value, ("dp", "tp"), pairs)


def sibling(value):
    return lax.ppermute(value, "tp", [(0, 1), (1, 0)])


def request_table(meta, holder, slot, ranks, cap, width):
    count = holder.shape[1]

    def body(meta_ref, h_ref, s_ref, out_ref):
        hrow = jnp.broadcast_to(h_ref[...], (count, count))
        srow = jnp.broadcast_to(s_ref[...], (count, count))
        i, j = iota((count, count), 0), iota((count, count), 1)
        hcol = jnp.sum(jnp.where(i == j, hrow, 0), axis=1, keepdims=True)
        scol = jnp.sum(jnp.where(i == j, srow, 0), axis=1, keepdims=True)
        rank = jnp.sum(jnp.where((hrow == hcol) & (j < i), 1, 0), axis=1, keepdims=True)
        lane = hcol * cap + rank
        hit = jnp.where(iota((count, width), 1) == lane, scol + 1, 0)
        row = jnp.sum(hit, axis=0, keepdims=True)
        out_ref[...] = jnp.where(iota((ranks, width), 0) == meta_ref[0], row, 0)

    return call(body, 1, 2, [jax.ShapeDtypeStruct((ranks, width), jnp.int32)])(meta, holder, slot)


def prepare(pool, queries, heads):
    pages, page_width = pool.shape
    tokens = queries.shape[0]

    def body(pool_ref, q_ref, pool_out, qe_out, qo_out):
        for j in range(page_width // PAIR):
            b = j * PAIR
            pool_out[:, b : b + 512] = pool_ref[:, b : b + 512]
            pool_out[:, b + 512 : b + 1024] = pool_ref[:, b + 576 : b + 1088]
            pool_out[:, b + 1024 : b + 1152] = jnp.concatenate(
                [pool_ref[:, b + 512 : b + 576], pool_ref[:, b + 1088 : b + 1152]], axis=1
            )
        zero = jnp.zeros((tokens, ROTARY_WIDTH), bf16)
        for h in range(heads):
            b = h * WIDTH
            nope = q_ref[:, b : b + 512]
            rope = q_ref[:, b + 512 : b + 576]
            rows = slice(h * tokens, (h + 1) * tokens)
            qe_out[rows, 0:512] = nope
            qo_out[rows, 0:512] = nope
            qe_out[rows, 512:640] = jnp.concatenate([rope, zero], axis=1)
            qo_out[rows, 512:640] = jnp.concatenate([zero, rope], axis=1)

    q_shape = jax.ShapeDtypeStruct((heads * tokens, PADDED), bf16)
    return call(body, 0, 2, [jax.ShapeDtypeStruct(pool.shape, bf16), q_shape, q_shape])(pool, queries)


def stack_keys(page_ref, rows, page_width):
    pairs = page_width // PAIR
    even = jnp.concatenate([page_ref[rows, j * PAIR : j * PAIR + 512] for j in range(pairs)], axis=0)
    odd = jnp.concatenate([page_ref[rows, j * PAIR + 512 : j * PAIR + 1024] for j in range(pairs)], axis=0)
    rope = jnp.concatenate([page_ref[rows, j * PAIR + 1024 : j * PAIR + 1152] for j in range(pairs)], axis=0)
    return even, odd, rope


def dot_nt(a, b):
    return lax.dot_general(a, b, (((1,), (1,)), ((), ())), preferred_element_type=f32)


def decode(lens, pool, qe):
    rows, heads, _ = qe.shape
    pages, page_width = pool.shape
    per_row = pages // rows
    pairs = page_width // PAIR

    def body(len_ref, pool_ref, q_ref, out_ref):
        key_rows = pairs * per_row
        s = iota((heads, key_rows), 1)
        pos = (s % per_row) * (2 * pairs) + 2 * (s // per_row)
        zero = jnp.zeros((heads, ROTARY_WIDTH), bf16)
        for g in range(rows):
            even, odd, rope = stack_keys(pool_ref, slice(g * per_row, (g + 1) * per_row), page_width)
            nope_q = q_ref[g, :, 0:512]
            rope_q = q_ref[g, :, 512:576]
            re = jnp.concatenate([rope_q, zero], axis=1)
            ro = jnp.concatenate([zero, rope_q], axis=1)
            se = dot_nt(nope_q, even) + dot_nt(re, rope)
            so = dot_nt(nope_q, odd) + dot_nt(ro, rope)
            se = jnp.where(pos < len_ref[g], se, masked_score)
            so = jnp.where(pos + 1 < len_ref[g], so, masked_score)
            peak = jnp.maximum(jnp.max(se, axis=1, keepdims=True), jnp.max(so, axis=1, keepdims=True))
            pe = jnp.exp2((se - peak) * exp2_scale)
            po = jnp.exp2((so - peak) * exp2_scale)
            den = jnp.sum(pe, axis=1, keepdims=True) + jnp.sum(po, axis=1, keepdims=True)
            out = jnp.dot(pe.astype(bf16), even, preferred_element_type=f32)
            out += jnp.dot(po.astype(bf16), odd, preferred_element_type=f32)
            out_ref[g] = (out / den).astype(bf16)

    return call(body, 1, 2, [jax.ShapeDtypeStruct((rows, heads, LATENT_WIDTH), bf16)])(lens, pool, qe)


def gather_pages(meta, table, pool, suffix, streams, cap, orders):
    ranks, width = table.shape
    pages, page_width = pool.shape
    block = TEAM * cap

    def body(meta_ref, table_ref, pool_ref, suffix_ref, *outs):
        me, core = meta_ref[0], meta_ref[1]
        team, member = me // TEAM, me % TEAM
        tab = table_ref[...].astype(f32).astype(bf16)
        for n, (base, half) in enumerate(streams):
            out_ref, bias_ref = outs[2 * n], outs[2 * n + 1]
            g = core * half + iota((half, ranks), 0)
            source = (team ^ (base + g // block)) * TEAM + (g % block) // cap
            pick = jnp.where(iota((half, ranks), 1) == source, 1.0, 0.0).astype(bf16)
            spread = jnp.dot(pick, tab, preferred_element_type=f32)
            g = core * half + iota((half, width), 0)
            mine = iota((half, width), 1) == me * cap + g % cap
            slot = jnp.sum(jnp.where(mine, spread, 0.0), axis=1, keepdims=True)
            hot = jnp.where(iota((half, pages), 1) + 1 == slot.astype(jnp.int32), 1.0, 0.0).astype(bf16)
            rows = jnp.dot(hot, pool_ref[...], preferred_element_type=f32).astype(bf16)
            out_ref[:, 0:page_width] = rows
            if n == 0:
                left = suffix_ref[:, 0:SUFFIX_LANES]
                right = suffix_ref[:, SUFFIX_LANES : 2 * SUFFIX_LANES]
                out_ref[:, page_width:] = jnp.zeros((half, SUFFIX_LANES), bf16)
                out_ref[0 : left.shape[0], page_width:] = jnp.where(core == 0, left, right)
            total = TEAM * half
            for side in range(2):
                owner = (core + side) % 2
                p = iota((width, total), 1)
                b, i = p // half, p % half
                first = jnp.where(owner == 0, orders[n][0][0], orders[n][1][0])
                second = jnp.where(owner == 0, orders[n][0][1], orders[n][1][1])
                third = jnp.where(owner == 0, orders[n][0][2], orders[n][1][2])
                away = (b % 2) * first + ((b // 2) % 2) * second + (b // 4) * third
                g = owner * half + i
                holder = (team ^ (base + g // block)) * TEAM + (member ^ away)
                sel = jnp.where(iota((width, total), 0) == holder * cap + g % cap, 1.0, 0.0).astype(bf16)
                q = iota((ranks, total), 1)
                asker = team * TEAM + ((owner * half + q % half) % block) // cap
                found = jnp.dot(tab, sel, preferred_element_type=f32)
                found = jnp.sum(jnp.where(iota((ranks, total), 0) == asker, found, 0.0), axis=0, keepdims=True)
                bias_ref[side : side + 1, :] = jnp.where(found > 0.0, 0.0, masked_score)

    outs = []
    for n, (base, half) in enumerate(streams):
        outs.append(jax.ShapeDtypeStruct((half, page_width + (SUFFIX_LANES if n == 0 else 0)), bf16))
        outs.append(jax.ShapeDtypeStruct((2, TEAM * half), f32))
    return call(body, 1, 3, outs)(meta, table, pool, suffix)


def softmax_step(q_rows, keys, bias, values, rows, m_ref, l_ref, acc_ref):
    scores = jnp.concatenate([dot_nt(q[rows, :], k) for q, k in keys], axis=1) + bias
    old = m_ref[rows, :]
    peak = jnp.maximum(old, jnp.max(scores, axis=1, keepdims=True))
    powers = jnp.exp2((scores - peak[:, 0:1]) * exp2_scale)
    factor = jnp.exp2((old - peak) * exp2_scale)
    m_ref[rows, :] = peak
    l_ref[rows, :] = l_ref[rows, :] * factor + jnp.sum(powers, axis=1, keepdims=True)
    add = jnp.dot(powers.astype(bf16), values, preferred_element_type=f32)
    acc_ref[rows, :] = acc_ref[rows, :] * factor[:, 0:1] + add


def attend(state, qe, qo, parts, page_width, row_block, last=None):
    n = len(parts)
    total = qe.shape[0]
    first = state is None

    def body(*refs):
        refs = list(refs)
        meta_ref = refs.pop(0) if last else None
        qe_ref, qo_ref = refs[0], refs[1]
        page_refs, bias_refs = refs[2 : 2 + n], refs[2 + n : 2 + 2 * n]
        refs = refs[2 + 2 * n :]
        if not first:
            m_in, l_in, acc_in = refs[:3]
            refs = refs[3:]
        if last:
            out_ref, m_ref, l_ref, acc_ref = refs
        else:
            m_ref, l_ref, acc_ref = refs
        if first:
            m_ref[...] = jnp.full(m_ref.shape, masked_score, f32)
            l_ref[...] = jnp.zeros(l_ref.shape, f32)
            acc_ref[...] = jnp.zeros(acc_ref.shape, f32)
        elif last:
            m_ref[...] = m_in[...]
            l_ref[...] = l_in[...]
            acc_ref[...] = acc_in[...]
        else:
            m_ref[...] = m_in[...]
            l_ref[...] = l_in[...]
            acc_ref[...] = acc_in[...]
        for page_ref, bias_ref in zip(page_refs, bias_refs):
            count = page_ref.shape[0]
            step = min(count, 64)
            for at in range(0, count, step):
                even, odd, rope = stack_keys(page_ref, slice(at, at + step), page_width)
                ke = jnp.concatenate([even, rope], axis=1)
                ko = jnp.concatenate([odd, rope], axis=1)
                values = jnp.concatenate([even, odd], axis=0)
                bias = jnp.concatenate([bias_ref[:, at : at + step]] * (page_width // WIDTH), axis=1)
                for r in range(0, total, row_block):
                    softmax_step(None, [(qe_ref, ke), (qo_ref, ko)], bias, values, slice(r, r + row_block), m_ref, l_ref, acc_ref)
        if last:
            _, tokens, heads = last
            live = iota((tokens, LATENT_WIDTH), 0) < meta_ref[2]
            for h in range(heads):
                rows = slice(h * tokens, (h + 1) * tokens)
                out = acc_ref[rows, :] / l_ref[rows, 0:1]
                out_ref[:, h * LATENT_WIDTH : (h + 1) * LATENT_WIDTH] = jnp.where(live, out, 0.0).astype(bf16)

    stat = jax.ShapeDtypeStruct((total, LANES), f32)
    acc = jax.ShapeDtypeStruct((total, LATENT_WIDTH), f32)
    pages = [p for p, _ in parts]
    biases = [b for _, b in parts]
    carried = [] if first else list(state)
    n_in = 2 + 2 * n + len(carried)
    if last:
        meta, tokens, heads = last
        out = jax.ShapeDtypeStruct((tokens, heads * LATENT_WIDTH), bf16)
        scratch = [pltpu.VMEM((total, LANES), f32), pltpu.VMEM((total, LANES), f32), pltpu.VMEM((total, LATENT_WIDTH), f32)]
        return call(body, 1, n_in, [out], scratch_shapes=scratch)(meta, qe, qo, *pages, *biases, *carried)
    return call(body, 0, n_in, [stat, stat, acc])(qe, qo, *pages, *biases, *carried)


def attend_suffix(state, meta, qe, arrivals, orders, page_width, tokens, row_block):
    total = qe.shape[0]
    first = state is None
    share = tokens // TEAM
    lanes = (PADDED - SUFFIX_LANES)

    def body(meta_ref, qe_ref, own0, own1, sib0, sib1, *refs):
        if first:
            m_ref, l_ref, acc_ref, key_ref = refs
            m_ref[...] = jnp.full(m_ref.shape, masked_score, f32)
            l_ref[...] = jnp.zeros(l_ref.shape, f32)
            acc_ref[...] = jnp.zeros(acc_ref.shape, f32)
        else:
            m_in, l_in, acc_in, m_ref, l_ref, acc_ref, key_ref = refs
            m_ref[...] = m_in[...]
            l_ref[...] = l_in[...]
            acc_ref[...] = acc_in[...]
        member, core = meta_ref[0] % TEAM, meta_ref[1]
        half = own0.shape[0] // 4
        for side, (low, high) in enumerate(((own0, own1), (sib0, sib1))):
            owner = (core + side) % 2
            for b in range(TEAM):
                masks = [
                    sum(o[k] for k in range(3) if (b >> k) & 1) for o in orders
                ]
                away = jnp.where(owner == 0, masks[0], masks[1])
                source = member ^ away
                src = low if b < 4 else high
                at = (b % 4) * half
                piece = src[at : at + share, page_width:]
                dst = pl.ds(pl.multiple_of(source * share, share), share)

                @pl.when(owner == 0)
                def _():
                    key_ref[dst, 0:SUFFIX_LANES] = piece

                @pl.when(owner == 1)
                def _():
                    key_ref[dst, SUFFIX_LANES:PADDED] = piece[:, 0:lanes]

        keys = key_ref[...]
        values = key_ref[:, 0:LATENT_WIDTH]
        u = iota((row_block, tokens), 1)
        for r in range(0, total, row_block):
            t = iota((row_block, tokens), 0) % tokens
            ok = (u <= t) & (u < meta_ref[2])
            bias = jnp.where(ok, 0.0, masked_score)
            softmax_step(None, [(qe_ref, keys)], bias, values, slice(r, r + row_block), m_ref, l_ref, acc_ref)

    stat = jax.ShapeDtypeStruct((total, LANES), f32)
    acc = jax.ShapeDtypeStruct((total, LATENT_WIDTH), f32)
    carried = [] if first else list(state)
    return call(body, 1, 5 + len(carried), [stat, stat, acc], scratch_shapes=[pltpu.VMEM((tokens, PADDED), bf16)])(
        meta, qe, *arrivals, *carried
    )


def shards(pool, page_holder, page_slot, suffix_latent_rows, prefill_queries, suffix_len, decode_queries, decode_len):
    ranks = lax.axis_size("dp")
    me = lax.axis_index("dp")
    core = lax.axis_index("tp")
    teams = ranks // TEAM
    pull = page_holder.shape[0]
    cap = (pull + ranks - 1) // ranks
    width = -(-ranks * cap // LANES) * LANES
    page_width = pool.shape[1]
    tokens = prefill_queries.shape[1]
    heads = prefill_queries.shape[2] // WIDTH
    share = suffix_latent_rows.shape[1] // WIDTH
    length = lax.dynamic_index_in_dim(suffix_len, me // TEAM, keepdims=False)
    meta = jnp.stack([me.astype(jnp.int32), core.astype(jnp.int32), length])

    table = request_table(meta, page_holder.reshape(1, -1), page_slot.reshape(1, -1), ranks, cap, width)
    step = 1
    while step < ranks:
        table = table + xperm(table, (step, step))
        step *= 2

    paged, qe, qo = prepare(pool, prefill_queries[0], heads)
    dq = decode_queries.reshape(decode_queries.shape[0], -1, WIDTH)
    decode_part = decode(decode_len, paged, dq).reshape(decode_queries.shape[0], -1)

    suffix = jnp.pad(suffix_latent_rows.reshape(share, WIDTH), ((0, 0), (0, 2 * SUFFIX_LANES - WIDTH)))

    block = TEAM * cap
    if block % 32 == 0:
        streams = [(j, block // 2) for j in range(teams)]
    else:
        streams = [(0, teams * block // 2)]
    orders = [((4, 2, 1), (1, 2, 4)), ((4, 2, 1), (1, 4, 2))]
    orders = [orders[n % 2] for n in range(len(streams))]
    sent = gather_pages(meta, table, paged, suffix, streams, cap, orders)

    parts = []
    state = None
    first_arrivals = None
    for n, (base, half) in enumerate(streams):
        rows, bias = sent[2 * n], sent[2 * n + 1]
        unit = min(block, half)
        pieces = []
        for at in range(0, half, unit):
            masks = tuple(TEAM * (base + (c * half + at) // block) for c in range(2))
            piece = rows[at : at + unit, :page_width] if half > unit else rows
            pieces.append(xperm(piece, masks) if any(masks) else piece)
        if half > unit:
            rows = jnp.concatenate([jnp.concatenate(pieces, axis=0), rows[:, page_width:]], axis=1)
        else:
            rows = pieces[0]
        masks = list(zip(*orders[n]))
        got = xperm(rows, masks[0])
        low = jnp.concatenate([rows, got], axis=0)
        low = jnp.concatenate([low, xperm(low, masks[1])], axis=0)
        high = xperm(low, masks[2])
        low_sib = sibling(low)
        high_sib = sibling(high)
        cut = 4 * half
        if n == 0:
            first_arrivals = (low, high, low_sib, high_sib)
        parts.append([(low, bias[0:1, :cut]), (low_sib, bias[1:2, :cut])])
        parts.append([(high, bias[0:1, cut:]), (high_sib, bias[1:2, cut:])])
    row_block = 128
    for n, group in enumerate(parts):
        if n == len(parts) - 1:
            out = attend(state, qe, qo, group, page_width, row_block, last=(meta, tokens, heads))
        else:
            state = attend(state, qe, qo, group, page_width, row_block)
        if n == 1 or len(parts) == 1:
            pass
        if n == 0:
            state = attend_suffix(state, meta, qe, first_arrivals, orders[0], page_width, tokens, row_block)
    return (out[None], decode_part)


def solution(mesh):
    placed = (
        P(("groups", "dp"), None),
        P(("groups", "dp")),
        P(("groups", "dp")),
        P(("groups", "dp"), None),
        P(("groups", "dp"), None, "tp"),
        P("groups"),
        P(("groups", "dp"), "tp"),
        P(("groups", "dp")),
    )
    return jax.shard_map(
        shards,
        mesh=mesh,
        in_specs=placed,
        out_specs=(P(("groups", "dp"), None, "tp"), P(("groups", "dp"), "tp")),
        check_vma=False,
    )
```

```python
import math

import jax
import jax.numpy as jnp
from jax import lax
from jax.experimental import pallas as pl
from jax.experimental.pallas import tpu as pltpu
from jax.sharding import PartitionSpec as P

LATENT_WIDTH = 512
ROTARY_WIDTH = 64
WIDTH = LATENT_WIDTH + ROTARY_WIDTH
PADDED = 640
PAIR = 2 * WIDTH
TEAM = 8
LANES = 128
SUFFIX_LANES = 384

softmax_scale = 192.0 ** (-0.5)
exp2_scale = softmax_scale * math.log2(math.e)
masked_score = -1e30


f32 = jnp.float32
bf16 = jnp.bfloat16


def iota(shape, dim):
    return lax.broadcasted_iota(jnp.int32, shape, dim)


def vmem():
    return pl.BlockSpec(memory_space=pltpu.VMEM)


def smem():
    return pl.BlockSpec(memory_space=pltpu.SMEM)


def call(body, n_smem, n_in, outs, mib=12, **kw):
    return pl.pallas_call(
        body,
        in_specs=[smem()] * n_smem + [vmem()] * n_in,
        out_specs=tuple(vmem() for _ in outs) if len(outs) > 1 else vmem(),
        out_shape=tuple(outs) if len(outs) > 1 else outs[0],
        compiler_params=pltpu.CompilerParams(vmem_limit_bytes=mib << 20),
        **kw,
    )


def xperm(value, masks):
    n, cores = lax.axis_size("dp"), lax.axis_size("tp")
    pairs = [(d * cores + c, (d ^ masks[c % 2]) * cores + c) for d in range(n) for c in range(cores)]
    return lax.ppermute(value, ("dp", "tp"), pairs)


def sibling(value):
    return lax.ppermute(value, "tp", [(0, 1), (1, 0)])


def request_table(holder, slot, ranks, cap, width):
    count = holder.shape[1]

    def body(h_ref, s_ref, out_ref):
        hrow = jnp.broadcast_to(h_ref[...], (count, count))
        srow = jnp.broadcast_to(s_ref[...], (count, count))
        i, j = iota((count, count), 0), iota((count, count), 1)
        hcol = jnp.sum(jnp.where(i == j, hrow, 0), axis=1, keepdims=True)
        scol = jnp.sum(jnp.where(i == j, srow, 0), axis=1, keepdims=True)
        rank = jnp.sum(jnp.where((hrow == hcol) & (j < i), 1, 0), axis=1, keepdims=True)
        lane = hcol * cap + rank
        hit = jnp.where(iota((count, width), 1) == lane, scol + 1, 0)
        row = jnp.sum(hit, axis=0, keepdims=True)
        out_ref[...] = jnp.where(iota((ranks, width), 0) == lax.axis_index("dp"), row, 0)

    return call(body, 0, 2, [jax.ShapeDtypeStruct((ranks, width), jnp.int32)])(holder, slot)


def paired(page, page_width):
    out = []
    for b in range(0, page_width, PAIR):
        out.append(page[:, b : b + 512])
        out.append(page[:, b + 576 : b + 1088])
        out.append(jnp.concatenate([page[:, b + 512 : b + 576], page[:, b + 1088 : b + 1152]], axis=1))
    return jnp.concatenate(out, axis=1)


def prepare(queries, heads):
    tokens = queries.shape[0]

    def body(q_ref, qe_out, qo_out):
        zero = jnp.zeros((tokens, ROTARY_WIDTH), bf16)
        for h in range(heads):
            b = h * WIDTH
            nope = q_ref[:, b : b + 512]
            rope = q_ref[:, b + 512 : b + 576]
            rows = slice(h * tokens, (h + 1) * tokens)
            qe_out[rows, 0:512] = nope
            qo_out[rows, 0:512] = nope
            qe_out[rows, 512:640] = jnp.concatenate([rope, zero], axis=1)
            qo_out[rows, 512:640] = jnp.concatenate([zero, rope], axis=1)

    q_shape = jax.ShapeDtypeStruct((heads * tokens, PADDED), bf16)
    return call(body, 0, 1, [q_shape, q_shape])(queries)


def stack_keys(page_ref, rows, page_width):
    pairs = page_width // PAIR
    even = jnp.concatenate([page_ref[rows, j * PAIR : j * PAIR + 512] for j in range(pairs)], axis=0)
    odd = jnp.concatenate([page_ref[rows, j * PAIR + 512 : j * PAIR + 1024] for j in range(pairs)], axis=0)
    rope = jnp.concatenate([page_ref[rows, j * PAIR + 1024 : j * PAIR + 1152] for j in range(pairs)], axis=0)
    return even, odd, rope


def dot_nt(a, b):
    return lax.dot_general(a, b, (((1,), (1,)), ((), ())), preferred_element_type=f32)


def decode(lens, pool, qe):
    rows, heads, _ = qe.shape
    pages, page_width = pool.shape
    per_row = pages // rows
    pairs = page_width // PAIR

    def body(len_ref, pool_ref, q_ref, out_ref):
        key_rows = pairs * per_row
        s = iota((heads, key_rows), 1)
        pos = (s % per_row) * (2 * pairs) + 2 * (s // per_row)
        zero = jnp.zeros((heads, ROTARY_WIDTH), bf16)
        for g in range(rows):
            even, odd, rope = stack_keys(paired(pool_ref[g * per_row : (g + 1) * per_row, :], page_width), slice(None), page_width)
            nope_q = q_ref[g, :, 0:512]
            rope_q = q_ref[g, :, 512:576]
            re = jnp.concatenate([rope_q, zero], axis=1)
            ro = jnp.concatenate([zero, rope_q], axis=1)
            se = dot_nt(nope_q, even) + dot_nt(re, rope)
            so = dot_nt(nope_q, odd) + dot_nt(ro, rope)
            se = jnp.where(pos < len_ref[g], se, masked_score)
            so = jnp.where(pos + 1 < len_ref[g], so, masked_score)
            peak = jnp.maximum(jnp.max(se, axis=1, keepdims=True), jnp.max(so, axis=1, keepdims=True))
            pe = jnp.exp2((se - peak) * exp2_scale)
            po = jnp.exp2((so - peak) * exp2_scale)
            den = jnp.sum(pe, axis=1, keepdims=True) + jnp.sum(po, axis=1, keepdims=True)
            out = jnp.dot(pe.astype(bf16), even, preferred_element_type=f32)
            out += jnp.dot(po.astype(bf16), odd, preferred_element_type=f32)
            out_ref[g] = (out / den).astype(bf16)

    return call(body, 1, 2, [jax.ShapeDtypeStruct((rows, heads, LATENT_WIDTH), bf16)])(lens, pool, qe)


def gather_pages(table, pool, suffix, streams, cap):
    ranks, width = table.shape
    pages, page_width = pool.shape
    block = TEAM * cap
    total = sum(half for _, half in streams)

    def body(table_ref, pool_ref, suffix_ref, *outs):
        me, core = lax.axis_index("dp"), lax.axis_index("tp")
        team = me // TEAM
        tab = table_ref[...].astype(f32).astype(bf16)

        def position(shape):
            n, row = iota(shape, 0), []
            g = jnp.zeros(shape, jnp.int32)
            base = jnp.zeros(shape, jnp.int32)
            at = 0
            for first, half in streams:
                inside = (n >= at) & (n < at + half)
                g = jnp.where(inside, n - at + core * half, g)
                base = jnp.where(inside, first, base)
                at += half
            return base, g

        base, g = position((total, ranks))
        source = (team ^ (base + g // block)) * TEAM + (g % block) // cap
        pick = jnp.where(iota((total, ranks), 1) == source, 1.0, 0.0).astype(bf16)
        spread = jnp.dot(pick, tab, preferred_element_type=f32)
        _, g = position((total, width))
        mine = iota((total, width), 1) == me * cap + g % cap
        slot = jnp.sum(jnp.where(mine, spread, 0.0), axis=1, keepdims=True)
        hot = jnp.where(iota((total, pages), 1) + 1 == slot.astype(jnp.int32), 1.0, 0.0).astype(bf16)
        rows = jnp.dot(hot, pool_ref[...], preferred_element_type=f32).astype(bf16)
        at = 0
        for n, (_, half) in enumerate(streams):
            outs[n][:, 0:page_width] = paired(rows[at : at + half], page_width)
            at += half
            if n == 0:
                left = suffix_ref[:, 0:SUFFIX_LANES]
                right = suffix_ref[:, SUFFIX_LANES : 2 * SUFFIX_LANES]
                if half > left.shape[0]:
                    outs[n][:, page_width:] = jnp.zeros((half, SUFFIX_LANES), bf16)
                outs[n][0 : left.shape[0], page_width:] = jnp.where(core == 0, left, right)

    outs = [
        jax.ShapeDtypeStruct((half, page_width + (SUFFIX_LANES if n == 0 else 0)), bf16)
        for n, (_, half) in enumerate(streams)
    ]
    out = call(body, 0, 3, outs)(table, pool, suffix)
    return out if len(outs) > 1 else (out,)


def key_masks(table, streams, cap, orders):
    ranks, width = table.shape
    block = TEAM * cap

    def body(table_ref, *outs):
        me, core = lax.axis_index("dp"), lax.axis_index("tp")
        team, member = me // TEAM, me % TEAM
        tab = table_ref[...].astype(f32).astype(bf16)
        for n, (base, half) in enumerate(streams):
            total = TEAM * half
            for side in range(2):
                owner = (core + side) % 2
                p = iota((width, total), 1)
                b, i = p // half, p % half
                away = jnp.zeros((width, total), jnp.int32)
                for k in range(3):
                    step = jnp.where(owner == 0, orders[n][0][k], orders[n][1][k])
                    away += ((b // (1 << k)) % 2) * step
                g = owner * half + i
                holder = (team ^ (base + g // block)) * TEAM + (member ^ away)
                sel = jnp.where(iota((width, total), 0) == holder * cap + g % cap, 1.0, 0.0).astype(bf16)
                q = iota((ranks, total), 1)
                asker = team * TEAM + ((owner * half + q % half) % block) // cap
                found = jnp.dot(tab, sel, preferred_element_type=f32)
                found = jnp.sum(jnp.where(iota((ranks, total), 0) == asker, found, 0.0), axis=0, keepdims=True)
                outs[n][side : side + 1, :] = jnp.where(found > 0.0, 0.0, masked_score)

    outs = [jax.ShapeDtypeStruct((2, TEAM * half), f32) for _, half in streams]
    out = call(body, 0, 1, outs)(table)
    return out if len(outs) > 1 else (out,)


CHUNK = 128


def softmax_step(s_ref, p_ref, width, bias, old_state, new_state, values, row_block):
    m_old, l_old, acc_old = old_state
    m_ref, l_ref, acc_ref = new_state
    total = s_ref.shape[0]
    for r in range(0, total, row_block):
        rows = slice(r, r + row_block)
        scores = s_ref[rows, 0:width] + (bias(r) if callable(bias) else bias)
        peak = jnp.max(scores, axis=1, keepdims=True)
        if m_old is None:
            peak = jnp.broadcast_to(peak, (row_block, LANES))
        else:
            peak = jnp.maximum(m_old[rows, :], peak)
        powers = jnp.exp2((scores - jnp.concatenate([peak] * (width // LANES), axis=1)) * exp2_scale)
        added = jnp.sum(powers, axis=1, keepdims=True)
        if m_old is None:
            l_ref[rows, :] = jnp.broadcast_to(added, (row_block, LANES))
        else:
            factor = jnp.exp2((m_old[rows, :] - peak) * exp2_scale)
            l_ref[rows, :] = l_old[rows, :] * factor + added
            acc_ref[rows, :] = acc_old[rows, :] * jnp.concatenate([factor] * (LATENT_WIDTH // LANES), axis=1)
        m_ref[rows, :] = peak
        p_ref[rows, 0:width] = powers.astype(bf16)
    add = jnp.dot(p_ref[:, 0:width], values, preferred_element_type=f32)
    if m_old is None:
        acc_ref[...] = add
    else:
        acc_ref[...] += add


def state_shapes(total):
    stat = jax.ShapeDtypeStruct((total, LANES), f32)
    return [stat, stat, jax.ShapeDtypeStruct((total, LATENT_WIDTH), f32)]


def attend(state, qe, qo, parts, page_width, row_block, last=None):
    n = len(parts)
    total = qe.shape[0]
    first = state is None
    pieces = []
    for k, (page, _) in enumerate(parts):
        step = min(page.shape[0], CHUNK // 2)
        pieces += [(k, at, step) for at in range(0, page.shape[0], step)]
    groups, size = [[]], 0
    for piece in pieces:
        if size + piece[2] > CHUNK:
            groups.append([])
            size = 0
        groups[-1].append(piece)
        size += piece[2]
    widest = max(sum(p[2] for p in g) for g in groups) * (page_width // WIDTH)

    def body(*refs):
        refs = list(refs)
        len_ref = refs.pop(0) if last else None
        qe_ref, qo_ref = refs[0], refs[1]
        page_refs, bias_refs = refs[2 : 2 + n], refs[2 + n : 2 + 2 * n]
        refs = refs[2 + 2 * n :]
        old = (None, None, None)
        if not first:
            old, refs = tuple(refs[:3]), refs[3:]
        if last:
            out_ref, refs = refs[0], refs[1:]
        new = tuple(refs[:3])
        s_ref, p_ref = refs[3:]
        for group in groups:
            at_col, biases, values = 0, [], []
            for k, at, step in group:
                even, odd, rope = stack_keys(page_refs[k], slice(at, at + step), page_width)
                for q_ref, key in ((qe_ref, even), (qo_ref, odd)):
                    width = key.shape[0]
                    s_ref[:, at_col : at_col + width] = dot_nt(q_ref[...], jnp.concatenate([key, rope], axis=1))
                    at_col += width
                    values.append(key)
                biases += [bias_refs[k][:, at : at + step]] * (page_width // WIDTH)
            softmax_step(
                s_ref, p_ref, at_col, jnp.concatenate(biases, axis=1), old, new, jnp.concatenate(values, axis=0), row_block
            )
            old = new
        if last:
            _, tokens, heads = last
            m_ref, l_ref, acc_ref = new
            length = len_ref[lax.axis_index("dp") // TEAM]
            live = iota((tokens, LATENT_WIDTH), 0) < length
            for h in range(heads):
                rows = slice(h * tokens, (h + 1) * tokens)
                den = jnp.concatenate([l_ref[rows, :]] * (LATENT_WIDTH // LANES), axis=1)
                out = jnp.where(live, acc_ref[rows, :] / den, 0.0).astype(bf16)
                out_ref[:, h * LATENT_WIDTH : (h + 1) * LATENT_WIDTH] = out

    pages = [p for p, _ in parts]
    biases = [b for _, b in parts]
    carried = [] if first else list(state)
    n_in = 2 + 2 * n + len(carried)
    scratch = [pltpu.VMEM((total, widest), f32), pltpu.VMEM((total, widest), bf16)]
    mib = 12 + (sum(p.size * 2 for p in pages) >> 20)
    if last:
        suffix_len, tokens, heads = last
        out = jax.ShapeDtypeStruct((tokens, heads * LATENT_WIDTH), bf16)
        scratch = [pltpu.VMEM(x.shape, f32) for x in state_shapes(total)] + scratch
        return call(body, 1, n_in, [out], mib, scratch_shapes=scratch)(suffix_len, qe, qo, *pages, *biases, *carried)
    return call(body, 0, n_in, state_shapes(total), mib, scratch_shapes=scratch)(qe, qo, *pages, *biases, *carried)


def attend_suffix(state, suffix_len, qe, arrivals, orders, page_width, tokens, row_block):
    total = qe.shape[0]
    first = state is None
    share = tokens // TEAM
    lanes = PADDED - SUFFIX_LANES

    def body(len_ref, qe_ref, own0, own1, sib0, sib1, *refs):
        old = (None, None, None)
        if not first:
            old, refs = tuple(refs[:3]), refs[3:]
        new = tuple(refs[:3])
        key_ref, s_ref, p_ref = refs[3:]
        me, core = lax.axis_index("dp"), lax.axis_index("tp")
        member = me % TEAM
        length = len_ref[me // TEAM]
        half = own0.shape[0] // 4
        for side, (low, high) in enumerate(((own0, own1), (sib0, sib1))):
            owner = (core + side) % 2
            for b in range(TEAM):
                masks = [sum(o[k] for k in range(3) if (b >> k) & 1) for o in orders]
                source = member ^ jnp.where(owner == 0, masks[0], masks[1])
                src = low if b < 4 else high
                at = (b % 4) * half
                piece = src[at : at + share, page_width:]
                dst = pl.ds(pl.multiple_of(source * share, share), share)

                @pl.when(owner == 0)
                def _():
                    key_ref[dst, 0:SUFFIX_LANES] = piece

                @pl.when(owner == 1)
                def _():
                    key_ref[dst, SUFFIX_LANES:PADDED] = piece[:, 0:lanes]

        s_ref[...] = dot_nt(qe_ref[...], key_ref[...])
        u = iota((row_block, tokens), 1)

        def bias(r):
            t = (iota((row_block, tokens), 0) + r) % tokens
            return jnp.where((u <= t) & (u < length), 0.0, masked_score)

        softmax_step(s_ref, p_ref, tokens, bias, old, new, key_ref[:, 0:LATENT_WIDTH], row_block)

    carried = [] if first else list(state)
    scratch = [
        pltpu.VMEM((tokens, PADDED), bf16),
        pltpu.VMEM((total, tokens), f32),
        pltpu.VMEM((total, tokens), bf16),
    ]
    return call(body, 1, 5 + len(carried), state_shapes(total), scratch_shapes=scratch)(
        suffix_len, qe, *arrivals, *carried
    )


def shards(pool, page_holder, page_slot, suffix_latent_rows, prefill_queries, suffix_len, decode_queries, decode_len):
    ranks = lax.axis_size("dp")
    teams = ranks // TEAM
    pull = page_holder.shape[0]
    cap = (pull + ranks - 1) // ranks
    width = -(-ranks * cap // LANES) * LANES
    page_width = pool.shape[1]
    tokens = prefill_queries.shape[1]
    heads = prefill_queries.shape[2] // WIDTH
    share = suffix_latent_rows.shape[1] // WIDTH

    table = request_table(page_holder.reshape(1, -1), page_slot.reshape(1, -1), ranks, cap, width)
    step = 1
    while step < ranks:
        table = table + xperm(table, (step, step))
        step *= 2

    qe, qo = prepare(prefill_queries[0], heads)
    dq = decode_queries.reshape(decode_queries.shape[0], -1, WIDTH)
    decode_part = decode(decode_len, pool, dq).reshape(decode_queries.shape[0], -1)

    suffix = jnp.pad(suffix_latent_rows.reshape(share, WIDTH), ((0, 0), (0, 2 * SUFFIX_LANES - WIDTH)))

    block = TEAM * cap
    if block % 32 == 0:
        streams = [(j, block // 2) for j in range(teams)]
    else:
        streams = [(0, teams * block // 2)]
    orders = [((4, 2, 1), (1, 4, 2))] * len(streams)
    sent = gather_pages(table, pool, suffix, streams, cap)
    masks_of = key_masks(table, streams, cap, orders)

    parts = []
    state = None
    first_arrivals = None
    for n, (base, half) in enumerate(streams):
        rows, bias = sent[n], masks_of[n]
        unit = min(block, half)
        pieces = []
        for at in range(0, half, unit):
            masks = tuple(TEAM * (base + (c * half + at) // block) for c in range(2))
            piece = rows[at : at + unit, :page_width] if half > unit else rows
            pieces.append(xperm(piece, masks) if any(masks) else piece)
        if half > unit:
            rows = jnp.concatenate([jnp.concatenate(pieces, axis=0), rows[:, page_width:]], axis=1)
        else:
            rows = pieces[0]
        masks = list(zip(*orders[n]))
        got = xperm(rows, masks[0])
        low = jnp.concatenate([rows, got], axis=0)
        low = jnp.concatenate([low, xperm(low, masks[1])], axis=0)
        high = xperm(low, masks[2])
        low_sib = sibling(low)
        high_sib = sibling(high)
        cut = 4 * half
        if n == 0:
            first_arrivals = (low, high, low_sib, high_sib)
        parts.append([(low, bias[0:1, :cut]), (low_sib, bias[1:2, :cut])])
        parts.append([(high, bias[0:1, cut:]), (high_sib, bias[1:2, cut:])])
    row_block = 128
    for n, group in enumerate(parts):
        if n == len(parts) - 1:
            out = attend(state, qe, qo, group, page_width, row_block, last=(suffix_len, tokens, heads))
        else:
            state = attend(state, qe, qo, group, page_width, row_block)
        if n == 0:
            state = attend_suffix(state, suffix_len, qe, first_arrivals, orders[0], page_width, tokens, row_block)
    return (out[None], decode_part)


def solution(mesh):
    placed = (
        P(("groups", "dp"), None),
        P(("groups", "dp")),
        P(("groups", "dp")),
        P(("groups", "dp"), None),
        P(("groups", "dp"), None, "tp"),
        P("groups"),
        P(("groups", "dp"), "tp"),
        P(("groups", "dp")),
    )
    return jax.shard_map(
        shards,
        mesh=mesh,
        in_specs=placed,
        out_specs=(P(("groups", "dp"), None, "tp"), P(("groups", "dp"), "tp")),
        check_vma=False,
    )
```

```python
import math

import jax
import jax.numpy as jnp
from jax import lax
from jax.experimental import pallas as pl
from jax.experimental.pallas import tpu as pltpu
from jax.sharding import PartitionSpec as P


LATENT_WIDTH = 512
ROTARY_WIDTH = 64
WIDTH = LATENT_WIDTH + ROTARY_WIDTH
PADDED = 640
PAIR = 2 * WIDTH
TEAM = 8
LANES = 128
SUFFIX_LANES = 384
CHUNK = 128

softmax_scale = 192.0 ** (-0.5)
exp2_scale = softmax_scale * math.log2(math.e)
masked_score = -1e30


f32 = jnp.float32
bf16 = jnp.bfloat16


def iota(shape, dim):
    return lax.broadcasted_iota(jnp.int32, shape, dim)


def vmem():
    return pl.BlockSpec(memory_space=pltpu.VMEM)


def smem():
    return pl.BlockSpec(memory_space=pltpu.SMEM)


def call(body, n_smem, n_in, outs, mib=12, **kw):
    return pl.pallas_call(
        body,
        in_specs=[smem()] * n_smem + [vmem()] * n_in,
        out_specs=tuple(vmem() for _ in outs) if len(outs) > 1 else vmem(),
        out_shape=tuple(outs) if len(outs) > 1 else outs[0],
        compiler_params=pltpu.CompilerParams(vmem_limit_bytes=mib << 20),
        **kw,
    )


def xperm(value, masks):
    n, cores = lax.axis_size("dp"), lax.axis_size("tp")
    pairs = [(d * cores + c, (d ^ masks[c % 2]) * cores + c) for d in range(n) for c in range(cores)]
    return lax.ppermute(value, ("dp", "tp"), pairs)


def sibling(value):
    return lax.ppermute(value, "tp", [(0, 1), (1, 0)])


def request_table(holder, slot, ranks, cap, width):
    count = holder.shape[1]

    def body(h_hbm, s_hbm, out_ref, h_ref, s_ref, sems):
        copies = [
            pltpu.make_async_copy(h_hbm, h_ref, sems.at[0]),
            pltpu.make_async_copy(s_hbm, s_ref, sems.at[1]),
        ]
        for copy in copies:
            copy.start()
        for copy in copies:
            copy.wait()
        hrow = jnp.broadcast_to(h_ref[...], (count, count))
        srow = jnp.broadcast_to(s_ref[...], (count, count))
        i, j = iota((count, count), 0), iota((count, count), 1)
        hcol = jnp.sum(jnp.where(i == j, hrow, 0), axis=1, keepdims=True)
        scol = jnp.sum(jnp.where(i == j, srow, 0), axis=1, keepdims=True)
        rank = jnp.sum(jnp.where((hrow == hcol) & (j < i), 1, 0), axis=1, keepdims=True)
        lane = hcol * cap + rank
        hit = jnp.where(iota((count, width), 1) == lane, scol + 1, 0)
        row = jnp.sum(hit, axis=0, keepdims=True)
        out_ref[...] = jnp.where(iota((ranks, width), 0) == lax.axis_index("dp"), row, 0)

    return pl.pallas_call(
        body,
        in_specs=[pl.BlockSpec(memory_space=pltpu.HBM)] * 2,
        out_specs=vmem(),
        out_shape=jax.ShapeDtypeStruct((ranks, width), jnp.int32),
        scratch_shapes=[
            pltpu.VMEM((1, count), jnp.int32),
            pltpu.VMEM((1, count), jnp.int32),
            pltpu.SemaphoreType.DMA((2,)),
        ],
        compiler_params=pltpu.CompilerParams(vmem_limit_bytes=4 << 20),
    )(holder, slot)


def paired(page, page_width):
    out = []
    for b in range(0, page_width, PAIR):
        out.append(page[:, b : b + 512])
        out.append(page[:, b + 576 : b + 1088])
        out.append(jnp.concatenate([page[:, b + 512 : b + 576], page[:, b + 1088 : b + 1152]], axis=1))
    return jnp.concatenate(out, axis=1)


def prepare(queries, heads):
    tokens = queries.shape[0]

    def body(q_ref, qe_out, qo_out):
        zero = jnp.zeros((tokens, ROTARY_WIDTH), bf16)
        for h in range(heads):
            b = h * WIDTH
            nope = q_ref[:, b : b + 512]
            rope = q_ref[:, b + 512 : b + 576]
            rows = slice(h * tokens, (h + 1) * tokens)
            qe_out[rows, 0:512] = nope
            qo_out[rows, 0:512] = nope
            qe_out[rows, 512:640] = jnp.concatenate([rope, zero], axis=1)
            qo_out[rows, 512:640] = jnp.concatenate([zero, rope], axis=1)

    q_shape = jax.ShapeDtypeStruct((heads * tokens, PADDED), bf16)
    return call(body, 0, 1, [q_shape, q_shape])(queries)


def pair_pool(pool):
    def body(pool_ref, out_ref):
        out_ref[...] = paired(pool_ref[...], pool_ref.shape[1])

    return call(body, 0, 1, [jax.ShapeDtypeStruct(pool.shape, bf16)])(pool)


def stack_keys(page_ref, rows, page_width):
    pairs = page_width // PAIR
    even = jnp.concatenate([page_ref[rows, j * PAIR : j * PAIR + 512] for j in range(pairs)], axis=0)
    odd = jnp.concatenate([page_ref[rows, j * PAIR + 512 : j * PAIR + 1024] for j in range(pairs)], axis=0)
    rope = jnp.concatenate([page_ref[rows, j * PAIR + 1024 : j * PAIR + 1152] for j in range(pairs)], axis=0)
    return even, odd, rope


def dot_nt(a, b):
    return lax.dot_general(a, b, (((1,), (1,)), ((), ())), preferred_element_type=f32)


def decode(lens, pool, qe):
    rows, heads, _ = qe.shape
    pages, page_width = pool.shape
    per_row = pages // rows
    pairs = page_width // PAIR

    def body(len_ref, pool_ref, q_ref, out_ref):
        key_rows = pairs * per_row
        s = iota((heads, key_rows), 1)
        pos = (s % per_row) * (2 * pairs) + 2 * (s // per_row)
        zero = jnp.zeros((heads, ROTARY_WIDTH), bf16)
        done = []
        for g in range(rows):
            even, odd, rope = stack_keys(pool_ref, slice(g * per_row, (g + 1) * per_row), page_width)
            nope_q = q_ref[g, :, 0:512]
            rope_q = q_ref[g, :, 512:576]
            re = jnp.concatenate([rope_q, zero], axis=1)
            ro = jnp.concatenate([zero, rope_q], axis=1)
            se = dot_nt(nope_q, even) + dot_nt(re, rope)
            so = dot_nt(nope_q, odd) + dot_nt(ro, rope)
            se = jnp.where(pos < len_ref[g], se, masked_score)
            so = jnp.where(pos + 1 < len_ref[g], so, masked_score)
            peak = jnp.maximum(jnp.max(se, axis=1, keepdims=True), jnp.max(so, axis=1, keepdims=True))
            pe = jnp.exp2((se - peak) * exp2_scale)
            po = jnp.exp2((so - peak) * exp2_scale)
            den = jnp.sum(pe, axis=1, keepdims=True) + jnp.sum(po, axis=1, keepdims=True)
            out = jnp.dot(pe.astype(bf16), even, preferred_element_type=f32)
            out += jnp.dot(po.astype(bf16), odd, preferred_element_type=f32)
            done.append((out / den).astype(bf16))
        i, j = iota((rows * heads, rows * heads), 0), iota((rows * heads, rows * heads), 1)
        swap = jnp.where(j == (i % rows) * heads + i // rows, 1.0, 0.0).astype(bf16)
        done = jnp.dot(swap, jnp.concatenate(done, axis=0), preferred_element_type=f32)
        for h in range(heads):
            out_ref[:, h * LATENT_WIDTH : (h + 1) * LATENT_WIDTH] = done[h * rows : (h + 1) * rows, :].astype(bf16)

    return call(body, 1, 2, [jax.ShapeDtypeStruct((rows, heads * LATENT_WIDTH), bf16)])(lens, pool, qe)


def gather_pages(table, pool, suffix, streams, cap):
    ranks, width = table.shape
    pages, page_width = pool.shape
    block = TEAM * cap
    total = sum(half for _, half in streams)

    def body(table_ref, pool_ref, suffix_ref, *outs):
        me, core = lax.axis_index("dp"), lax.axis_index("tp")
        team = me // TEAM
        tab = table_ref[...].astype(f32).astype(bf16)

        def position(shape):
            n = iota(shape, 0)
            g = jnp.zeros(shape, jnp.int32)
            base = jnp.zeros(shape, jnp.int32)
            at = 0
            for first, half in streams:
                inside = (n >= at) & (n < at + half)
                g = jnp.where(inside, n - at + core * half, g)
                base = jnp.where(inside, first, base)
                at += half
            return base, g

        base, g = position((total, ranks))
        source = (team ^ (base + g // block)) * TEAM + (g % block) // cap
        pick = jnp.where(iota((total, ranks), 1) == source, 1.0, 0.0).astype(bf16)
        spread = jnp.dot(pick, tab, preferred_element_type=f32)
        _, g = position((total, width))
        mine = iota((total, width), 1) == me * cap + g % cap
        slot = jnp.sum(jnp.where(mine, spread, 0.0), axis=1, keepdims=True)
        hot = jnp.where(iota((total, pages), 1) + 1 == slot.astype(jnp.int32), 1.0, 0.0).astype(bf16)
        rows = jnp.dot(hot, pool_ref[...], preferred_element_type=f32).astype(bf16)
        at = 0
        for n, (_, half) in enumerate(streams):
            outs[n][:, 0:page_width] = rows[at : at + half]
            at += half
            if n == 0:
                left = suffix_ref[:, 0:SUFFIX_LANES]
                right = suffix_ref[:, SUFFIX_LANES : 2 * SUFFIX_LANES]
                if half > left.shape[0]:
                    outs[n][:, page_width:] = jnp.zeros((half, SUFFIX_LANES), bf16)
                outs[n][0 : left.shape[0], page_width:] = jnp.where(core == 0, left, right)

    outs = [
        jax.ShapeDtypeStruct((half, page_width + (SUFFIX_LANES if n == 0 else 0)), bf16)
        for n, (_, half) in enumerate(streams)
    ]
    out = call(body, 0, 3, outs)(table, pool, suffix)
    return out if len(outs) > 1 else (out,)


def key_masks(table, streams, cap, orders, tokens):
    ranks, width = table.shape
    block = TEAM * cap

    def body(table_ref, *outs):
        me, core = lax.axis_index("dp"), lax.axis_index("tp")
        team, member = me // TEAM, me % TEAM
        tab = table_ref[...].astype(f32).astype(bf16)
        for n, (base, half) in enumerate(streams):
            total = TEAM * half
            for side in range(2):
                owner = (core + side) % 2
                p = iota((width, total), 1)
                b, i = p // half, p % half
                away = jnp.zeros((width, total), jnp.int32)
                for k in range(3):
                    step = jnp.where(owner == 0, orders[n][0][k], orders[n][1][k])
                    away += ((b // (1 << k)) % 2) * step
                g = owner * half + i
                holder = (team ^ (base + g // block)) * TEAM + (member ^ away)
                sel = jnp.where(iota((width, total), 0) == holder * cap + g % cap, 1.0, 0.0).astype(bf16)
                q = iota((ranks, total), 1)
                asker = team * TEAM + ((owner * half + q % half) % block) // cap
                found = jnp.dot(tab, sel, preferred_element_type=f32)
                found = jnp.sum(jnp.where(iota((ranks, total), 0) == asker, found, 0.0), axis=0, keepdims=True)
                found = jnp.where(found > 0.0, 0.0, masked_score)
                for k in range(4):
                    wide = []
                    for at in range(k * 2 * half, (k + 1) * 2 * half, min(2 * half, CHUNK // 2)):
                        wide += [found[:, at : at + min(2 * half, CHUNK // 2)]] * tokens
                    outs[n][side * 4 + k : side * 4 + k + 1, :] = jnp.concatenate(wide, axis=1)

    outs = [jax.ShapeDtypeStruct((8, 2 * half * tokens), f32) for _, half in streams]
    out = call(body, 0, 1, outs)(table)
    return out if len(outs) > 1 else (out,)


def softmax_step(s_ref, p_ref, width, bias, causal, old_state, new_state, values, row_block):
    m_old, l_old, acc_old = old_state
    m_ref, l_ref, acc_ref = new_state
    total = s_ref.shape[0]
    for r in range(0, total, row_block):
        rows = slice(r, r + row_block)
        if causal is None:
            scores = s_ref[rows, 0:width] + bias
        else:
            plain = bias.shape[1]
            scores = jnp.concatenate([s_ref[rows, 0:plain] + bias, s_ref[rows, plain:width] + causal(r, row_block)], axis=1)
        peak = jnp.max(scores, axis=1, keepdims=True)
        if m_old is None:
            peak = jnp.broadcast_to(peak, (row_block, LANES))
        else:
            peak = jnp.maximum(m_old[rows, :], peak)
        powers = jnp.exp2((scores - jnp.concatenate([peak] * (width // LANES), axis=1)) * exp2_scale)
        added = jnp.sum(powers, axis=1, keepdims=True)
        if m_old is None:
            l_ref[rows, :] = jnp.broadcast_to(added, (row_block, LANES))
        else:
            factor = jnp.exp2((m_old[rows, :] - peak) * exp2_scale)
            l_ref[rows, :] = l_old[rows, :] * factor + added
            acc_ref[rows, :] = acc_old[rows, :] * jnp.concatenate([factor] * (LATENT_WIDTH // LANES), axis=1)
        m_ref[rows, :] = peak
        p_ref[rows, 0:width] = powers.astype(bf16)
    add = jnp.dot(p_ref[:, 0:width], values, preferred_element_type=f32)
    if m_old is None:
        acc_ref[...] = add
    else:
        acc_ref[...] += add


def state_shapes(total):
    stat = jax.ShapeDtypeStruct((total, LANES), f32)
    return [stat, stat, jax.ShapeDtypeStruct((total, LATENT_WIDTH), f32)]


def collect_suffix(key_ref, came, orders, page_width, share):
    core, member = lax.axis_index("tp"), lax.axis_index("dp") % TEAM
    half = came[0].shape[0] // 2
    for b in range(TEAM):
        rows = slice((b % 2) * half, (b % 2) * half + share)
        mine, theirs = came[b // 2][rows, page_width:], came[4 + b // 2][rows, page_width:]
        for side in range(2):
            piece = jnp.where(core == side, mine, theirs)
            source = member ^ sum(orders[side][k] for k in range(3) if (b >> k) & 1)
            at = pl.ds(pl.multiple_of(source * share, share), share)
            if side == 0:
                key_ref[at, 0:SUFFIX_LANES] = piece
            else:
                key_ref[at, SUFFIX_LANES:PADDED] = piece[:, 0 : PADDED - SUFFIX_LANES]


def attend(state, qe, qo, parts, page_width, row_block, suffix_len, tokens, suffix=None, last=None):
    n = len(parts)
    total = qe.shape[0]
    first = state is None
    per = page_width // WIDTH
    pieces = []
    for k, (page, _, _) in enumerate(parts):
        step = min(page.shape[0], CHUNK // 2)
        pieces += [(k, at, step) for at in range(0, page.shape[0], step)]
    groups, size = [[]], 0
    for piece in pieces:
        if size + piece[2] > CHUNK:
            groups.append([])
            size = 0
        groups[-1].append(piece)
        size += piece[2]
    widest = max(sum(p[2] for p in g) for g in groups) * per + (tokens if suffix else 0)
    n_came = 8 if suffix else 0

    def body(len_ref, qe_ref, qo_ref, *refs):
        page_refs, bias_refs, refs = refs[:n], refs[n : 2 * n], refs[2 * n :]
        came, refs = refs[:n_came], refs[n_came:]
        old = (None, None, None)
        if not first:
            old, refs = tuple(refs[:3]), refs[3:]
        if last:
            out_ref, refs = refs[0], refs[1:]
        new = tuple(refs[:3])
        s_ref, p_ref = refs[3:5]
        length = len_ref[lax.axis_index("dp") // TEAM]
        for number, group in enumerate(groups):
            evens, odds, ropes, even_bias, odd_bias = [], [], [], [], []
            for k, at, step in group:
                even, odd, rope = stack_keys(page_refs[k], slice(at, at + step), page_width)
                evens.append(even)
                odds.append(odd)
                ropes.append(rope)
                row, half_keys = parts[k][2], step * per // 2
                even_bias.append(bias_refs[k][row : row + 1, at * per : at * per + half_keys])
                odd_bias.append(bias_refs[k][row : row + 1, at * per + half_keys : at * per + 2 * half_keys])
            rope = jnp.concatenate(ropes, axis=0)
            even, odd = jnp.concatenate(evens, axis=0), jnp.concatenate(odds, axis=0)
            width = even.shape[0]
            s_ref[:, 0:width] = dot_nt(qe_ref[...], jnp.concatenate([even, rope], axis=1))
            s_ref[:, width : 2 * width] = dot_nt(qo_ref[...], jnp.concatenate([odd, rope], axis=1))
            width *= 2
            values, causal = [even, odd], None
            if suffix and number == len(groups) - 1:
                key_ref = refs[5]
                collect_suffix(key_ref, came, suffix[1], page_width, tokens // TEAM)
                s_ref[:, width : width + tokens] = dot_nt(qe_ref[...], key_ref[...])
                width += tokens
                values.append(key_ref[:, 0:LATENT_WIDTH])

                def causal(r, count):
                    u = iota((count, tokens), 1)
                    t = (iota((count, tokens), 0) + r) % tokens
                    return jnp.where((u <= t) & (u < length), 0.0, masked_score)

            bias = jnp.concatenate(even_bias + odd_bias, axis=1)
            softmax_step(s_ref, p_ref, width, bias, causal, old, new, jnp.concatenate(values, axis=0), row_block)
            old = new
        if last:
            _, l_ref, acc_ref = new
            live = iota((tokens, LATENT_WIDTH), 0) < length
            for h in range(last):
                rows = slice(h * tokens, (h + 1) * tokens)
                share = 1.0 / l_ref[rows, :]
                out = acc_ref[rows, :] * jnp.concatenate([share] * (LATENT_WIDTH // LANES), axis=1)
                out_ref[:, h * LATENT_WIDTH : (h + 1) * LATENT_WIDTH] = jnp.where(live, out, 0.0).astype(bf16)

    pages = [p for p, _, _ in parts]
    biases = [b for _, b, _ in parts]
    came = list(suffix[0]) if suffix else []
    carried = [] if first else list(state)
    n_in = 2 + 2 * n + len(came) + len(carried)
    scratch = [pltpu.VMEM((total, widest), f32), pltpu.VMEM((total, widest), bf16)]
    if suffix:
        scratch.append(pltpu.VMEM((tokens, PADDED), bf16))
    mib = 12 + (sum(p.size * 2 for p in pages + came) >> 20)
    outs = state_shapes(total)
    if last:
        scratch = [pltpu.VMEM(x.shape, f32) for x in outs] + scratch
        outs = [jax.ShapeDtypeStruct((tokens, last * LATENT_WIDTH), bf16)]
    return call(body, 1, n_in, outs, mib, scratch_shapes=scratch)(suffix_len, qe, qo, *pages, *biases, *came, *carried)


def program(pool, page_holder, page_slot, suffix_latent_rows, prefill_queries, suffix_len, decode_queries, decode_len):
    ranks = lax.axis_size("dp")
    teams = ranks // TEAM
    pull = page_holder.shape[0]
    cap = (pull + ranks - 1) // ranks
    width = -(-ranks * cap // LANES) * LANES
    page_width = pool.shape[1]
    tokens = prefill_queries.shape[1]
    heads = prefill_queries.shape[2] // WIDTH
    share = suffix_latent_rows.shape[1] // WIDTH

    table = request_table(page_holder.reshape(1, -1), page_slot.reshape(1, -1), ranks, cap, width)
    step = 1
    while step < ranks:
        table = table + xperm(table, (step, step))
        step *= 2

    qe, qo = prepare(prefill_queries[0], heads)
    pool = pair_pool(pool)
    dq = decode_queries.reshape(decode_queries.shape[0], -1, WIDTH)
    decode_part = decode(decode_len, pool, dq)

    suffix = jnp.pad(suffix_latent_rows.reshape(share, WIDTH), ((0, 0), (0, 2 * SUFFIX_LANES - WIDTH)))

    block = TEAM * cap
    if block % 32 == 0:
        streams = [(j, block // 2) for j in range(teams)]
    else:
        streams = [(0, teams * block // 2)]
    orders = [((1, 2, 4), (2, 4, 1)), ((4, 2, 1), (1, 4, 2))]
    orders = [orders[n % 2] for n in range(len(streams))]
    sent = gather_pages(table, pool, suffix, streams, cap)
    masks_of = key_masks(table, streams, cap, orders, page_width // WIDTH)

    came = []
    for n, (base, half) in enumerate(streams):
        rows = sent[n]
        unit = min(block, half)
        pieces = []
        for at in range(0, half, unit):
            masks = tuple(TEAM * (base + (c * half + at) // block) for c in range(2))
            piece = rows[at : at + unit, :page_width] if half > unit else rows
            pieces.append(xperm(piece, masks) if any(masks) else piece)
        if half > unit:
            rows = jnp.concatenate([jnp.concatenate(pieces, axis=0), rows[:, page_width:]], axis=1)
        else:
            rows = pieces[0]
        masks = list(zip(*orders[n]))
        got = xperm(rows, masks[0])
        both = jnp.concatenate([rows, got], axis=0)
        second = xperm(both, masks[1])
        third = xperm(both, masks[2])
        fourth = xperm(second, masks[2])
        own = [both, second, third, fourth]
        other = []
        for piece in own:
            other.append(sibling(piece))
        came.append((own, other))

    row_block = 128
    plan = []
    for n in range(len(streams)):
        own, other = came[n]
        piece = [[(own[k], masks_of[n], k), (other[k], masks_of[n], 4 + k)] for k in range(4)]
        plan.append((f"att{n}a", piece[0] + piece[1]))
        if n < len(streams) - 1:
            plan.append((f"att{n}b", piece[2] + piece[3]))
        else:
            plan.append((f"att{n}b", piece[2]))
            plan.append((f"att{n}c", piece[3]))
    tail = "att0b" if len(streams) > 1 else plan[-1][0]
    state = None
    for n, (name, group) in enumerate(plan):
        suffix = (came[0][0] + came[0][1], orders[0]) if name == tail else None
        last = heads if n == len(plan) - 1 else None
        state = attend(state, qe, qo, group, page_width, row_block, suffix_len, tokens, suffix, last)
    return (state[None], decode_part)


def solution(mesh):
    placed = (
        P(("groups", "dp"), None),
        P(("groups", "dp")),
        P(("groups", "dp")),
        P(("groups", "dp"), None),
        P(("groups", "dp"), None, "tp"),
        P("groups"),
        P(("groups", "dp"), "tp"),
        P(("groups", "dp")),
    )
    return jax.shard_map(
        program,
        mesh=mesh,
        in_specs=placed,
        out_specs=(P(("groups", "dp"), None, "tp"), P(("groups", "dp"), "tp")),
        check_vma=False,
    )
```

```python
import math

import jax
import jax.numpy as jnp
from jax import lax
from jax.experimental import pallas as pl
from jax.experimental.pallas import tpu as pltpu
from jax.sharding import PartitionSpec as P


LATENT_WIDTH = 512
ROTARY_WIDTH = 64
WIDTH = LATENT_WIDTH + ROTARY_WIDTH
PADDED = 640
PAIR = 2 * WIDTH
TEAM = 8
LANES = 128
SUFFIX_LANES = 384
CHUNK = 128

softmax_scale = 192.0 ** (-0.5)
exp2_scale = softmax_scale * math.log2(math.e)
masked_score = -1e30


f32 = jnp.float32
bf16 = jnp.bfloat16


def iota(shape, dim):
    return lax.broadcasted_iota(jnp.int32, shape, dim)


def vmem():
    return pl.BlockSpec(memory_space=pltpu.VMEM)


def smem():
    return pl.BlockSpec(memory_space=pltpu.SMEM)


def call(body, n_smem, n_in, outs, mib=12, **kw):
    return pl.pallas_call(
        body,
        in_specs=[smem()] * n_smem + [vmem()] * n_in,
        out_specs=tuple(vmem() for _ in outs) if len(outs) > 1 else vmem(),
        out_shape=tuple(outs) if len(outs) > 1 else outs[0],
        compiler_params=pltpu.CompilerParams(vmem_limit_bytes=mib << 20),
        **kw,
    )


def xperm(value, masks):
    n, cores = lax.axis_size("dp"), lax.axis_size("tp")
    pairs = [(d * cores + c, (d ^ masks[c % 2]) * cores + c) for d in range(n) for c in range(cores)]
    return lax.ppermute(value, ("dp", "tp"), pairs)


def sibling(value):
    return lax.ppermute(value, "tp", [(0, 1), (1, 0)])


def request_table(asked, ranks, cap, width):
    count = asked.shape[1]

    def body(asked_ref, out_ref):
        hrow = jnp.broadcast_to(asked_ref[0:1, :], (count, count))
        srow = jnp.broadcast_to(asked_ref[1:2, :], (count, count))
        i, j = iota((count, count), 0), iota((count, count), 1)
        hcol = jnp.sum(jnp.where(i == j, hrow, 0), axis=1, keepdims=True)
        scol = jnp.sum(jnp.where(i == j, srow, 0), axis=1, keepdims=True)
        rank = jnp.sum(jnp.where((hrow == hcol) & (j < i), 1, 0), axis=1, keepdims=True)
        lane = hcol * cap + rank
        hit = jnp.where(iota((count, width), 1) == lane, scol + 1, 0)
        row = jnp.sum(hit, axis=0, keepdims=True)
        out_ref[...] = jnp.where(iota((ranks, width), 0) == lax.axis_index("dp"), row, 0)

    return call(body, 0, 1, [jax.ShapeDtypeStruct((ranks, width), jnp.int32)], 4)(asked)


def paired(page, page_width):
    out = []
    for b in range(0, page_width, PAIR):
        out.append(page[:, b : b + 512])
        out.append(page[:, b + 576 : b + 1088])
        out.append(jnp.concatenate([page[:, b + 512 : b + 576], page[:, b + 1088 : b + 1152]], axis=1))
    return jnp.concatenate(out, axis=1)


def prepare(queries, heads):
    tokens = queries.shape[0]

    def body(q_ref, qe_out, qo_out):
        zero = jnp.zeros((tokens, ROTARY_WIDTH), bf16)
        for h in range(heads):
            b = h * WIDTH
            nope = q_ref[:, b : b + 512]
            rope = q_ref[:, b + 512 : b + 576]
            rows = slice(h * tokens, (h + 1) * tokens)
            qe_out[rows, 0:512] = nope
            qo_out[rows, 0:512] = nope
            qe_out[rows, 512:640] = jnp.concatenate([rope, zero], axis=1)
            qo_out[rows, 512:640] = jnp.concatenate([zero, rope], axis=1)

    q_shape = jax.ShapeDtypeStruct((heads * tokens, PADDED), bf16)
    return call(body, 0, 1, [q_shape, q_shape])(queries)


def pair_pool(pool):
    def body(pool_ref, out_ref):
        out_ref[...] = paired(pool_ref[...], pool_ref.shape[1])

    return call(body, 0, 1, [jax.ShapeDtypeStruct(pool.shape, bf16)])(pool)


def stack_keys(page_ref, rows, page_width):
    pairs = page_width // PAIR
    even = jnp.concatenate([page_ref[rows, j * PAIR : j * PAIR + 512] for j in range(pairs)], axis=0)
    odd = jnp.concatenate([page_ref[rows, j * PAIR + 512 : j * PAIR + 1024] for j in range(pairs)], axis=0)
    rope = jnp.concatenate([page_ref[rows, j * PAIR + 1024 : j * PAIR + 1152] for j in range(pairs)], axis=0)
    return even, odd, rope


def dot_nt(a, b):
    return lax.dot_general(a, b, (((1,), (1,)), ((), ())), preferred_element_type=f32)


def decode(lens, pool, qe):
    rows, heads, _ = qe.shape
    pages, page_width = pool.shape
    per_row = pages // rows
    pairs = page_width // PAIR

    def body(len_ref, pool_ref, q_ref, out_ref):
        key_rows = pairs * per_row
        s = iota((heads, key_rows), 1)
        pos = (s % per_row) * (2 * pairs) + 2 * (s // per_row)
        zero = jnp.zeros((heads, ROTARY_WIDTH), bf16)
        done = []
        for g in range(rows):
            even, odd, rope = stack_keys(pool_ref, slice(g * per_row, (g + 1) * per_row), page_width)
            nope_q = q_ref[g, :, 0:512]
            rope_q = q_ref[g, :, 512:576]
            re = jnp.concatenate([rope_q, zero], axis=1)
            ro = jnp.concatenate([zero, rope_q], axis=1)
            se = dot_nt(nope_q, even) + dot_nt(re, rope)
            so = dot_nt(nope_q, odd) + dot_nt(ro, rope)
            se = jnp.where(pos < len_ref[g], se, masked_score)
            so = jnp.where(pos + 1 < len_ref[g], so, masked_score)
            peak = jnp.maximum(jnp.max(se, axis=1, keepdims=True), jnp.max(so, axis=1, keepdims=True))
            pe = jnp.exp2((se - peak) * exp2_scale)
            po = jnp.exp2((so - peak) * exp2_scale)
            den = jnp.sum(pe, axis=1, keepdims=True) + jnp.sum(po, axis=1, keepdims=True)
            out = jnp.dot(pe.astype(bf16), even, preferred_element_type=f32)
            out += jnp.dot(po.astype(bf16), odd, preferred_element_type=f32)
            done.append((out / den).astype(bf16))
        i, j = iota((rows * heads, rows * heads), 0), iota((rows * heads, rows * heads), 1)
        swap = jnp.where(j == (i % rows) * heads + i // rows, 1.0, 0.0).astype(bf16)
        done = jnp.dot(swap, jnp.concatenate(done, axis=0), preferred_element_type=f32)
        for h in range(heads):
            out_ref[:, h * LATENT_WIDTH : (h + 1) * LATENT_WIDTH] = done[h * rows : (h + 1) * rows, :].astype(bf16)

    return call(body, 1, 2, [jax.ShapeDtypeStruct((rows, heads * LATENT_WIDTH), bf16)])(lens, pool, qe)


def gather_pages(table, pool, suffix, streams, cap):
    ranks, width = table.shape
    pages, page_width = pool.shape
    block = TEAM * cap
    total = sum(half for _, half in streams)

    def body(table_ref, pool_ref, *outs):
        if suffix is not None:
            suffix_ref, outs = outs[0], outs[1:]
        me, core = lax.axis_index("dp"), lax.axis_index("tp")
        team = me // TEAM
        tab = table_ref[...].astype(f32).astype(bf16)

        def position(shape):
            n = iota(shape, 0)
            g = jnp.zeros(shape, jnp.int32)
            base = jnp.zeros(shape, jnp.int32)
            at = 0
            for first, half in streams:
                inside = (n >= at) & (n < at + half)
                g = jnp.where(inside, n - at + core * half, g)
                base = jnp.where(inside, first, base)
                at += half
            return base, g

        base, g = position((total, ranks))
        source = (team ^ (base + g // block)) * TEAM + (g % block) // cap
        pick = jnp.where(iota((total, ranks), 1) == source, 1.0, 0.0).astype(bf16)
        spread = jnp.dot(pick, tab, preferred_element_type=f32)
        _, g = position((total, width))
        mine = iota((total, width), 1) == me * cap + g % cap
        slot = jnp.sum(jnp.where(mine, spread, 0.0), axis=1, keepdims=True)
        hot = jnp.where(iota((total, pages), 1) + 1 == slot.astype(jnp.int32), 1.0, 0.0).astype(bf16)
        rows = jnp.dot(hot, pool_ref[...], preferred_element_type=f32).astype(bf16)
        at = 0
        for n, (_, half) in enumerate(streams):
            outs[n][:, 0:page_width] = rows[at : at + half]
            at += half
            if suffix is not None and n == 0:
                left = suffix_ref[:, 0:SUFFIX_LANES]
                right = suffix_ref[:, SUFFIX_LANES : 2 * SUFFIX_LANES]
                if half > left.shape[0]:
                    outs[n][:, page_width:] = jnp.zeros((half, SUFFIX_LANES), bf16)
                outs[n][0 : left.shape[0], page_width:] = jnp.where(core == 0, left, right)

    outs = [
        jax.ShapeDtypeStruct((half, page_width + (SUFFIX_LANES if n == 0 and suffix is not None else 0)), bf16)
        for n, (_, half) in enumerate(streams)
    ]
    given = [table, pool] + ([] if suffix is None else [suffix])
    out = call(body, 0, len(given), outs)(*given)
    return out if len(outs) > 1 else (out,)


def key_masks(table, streams, cap, orders, tokens):
    ranks, width = table.shape
    block = TEAM * cap

    def body(table_ref, *outs):
        me, core = lax.axis_index("dp"), lax.axis_index("tp")
        team, member = me // TEAM, me % TEAM
        tab = table_ref[...].astype(f32).astype(bf16)
        for n, (base, half) in enumerate(streams):
            total = TEAM * half
            for side in range(2):
                owner = (core + side) % 2
                p = iota((width, total), 1)
                b, i = p // half, p % half
                away = jnp.zeros((width, total), jnp.int32)
                for k in range(3):
                    step = jnp.where(owner == 0, orders[n][0][k], orders[n][1][k])
                    away += ((b // (1 << k)) % 2) * step
                g = owner * half + i
                holder = (team ^ (base + g // block)) * TEAM + (member ^ away)
                sel = jnp.where(iota((width, total), 0) == holder * cap + g % cap, 1.0, 0.0).astype(bf16)
                q = iota((ranks, total), 1)
                asker = team * TEAM + ((owner * half + q % half) % block) // cap
                found = jnp.dot(tab, sel, preferred_element_type=f32)
                found = jnp.sum(jnp.where(iota((ranks, total), 0) == asker, found, 0.0), axis=0, keepdims=True)
                found = jnp.where(found > 0.0, 0.0, masked_score)
                for k in range(4):
                    wide = []
                    for at in range(k * 2 * half, (k + 1) * 2 * half, min(2 * half, CHUNK // 2)):
                        wide += [found[:, at : at + min(2 * half, CHUNK // 2)]] * tokens
                    outs[n][side * 4 + k : side * 4 + k + 1, :] = jnp.concatenate(wide, axis=1)

    outs = [jax.ShapeDtypeStruct((8, 2 * half * tokens), f32) for _, half in streams]
    out = call(body, 0, 1, outs)(table)
    return out if len(outs) > 1 else (out,)


def softmax_step(s_ref, p_ref, width, bias, causal, old_state, new_state, values, row_block):
    m_old, l_old, acc_old = old_state
    m_ref, l_ref, acc_ref = new_state
    total = s_ref.shape[0]
    for r in range(0, total, row_block):
        rows = slice(r, r + row_block)
        if causal is None:
            scores = s_ref[rows, 0:width] + bias
        else:
            plain = bias.shape[1]
            scores = jnp.concatenate([s_ref[rows, 0:plain] + bias, s_ref[rows, plain:width] + causal(r, row_block)], axis=1)
        peak = jnp.max(scores, axis=1, keepdims=True)
        if m_old is None:
            peak = jnp.broadcast_to(peak, (row_block, LANES))
        else:
            peak = jnp.maximum(m_old[rows, :], peak)
        powers = jnp.exp2((scores - jnp.concatenate([peak] * (width // LANES), axis=1)) * exp2_scale)
        added = jnp.sum(powers, axis=1, keepdims=True)
        if m_old is None:
            l_ref[rows, :] = jnp.broadcast_to(added, (row_block, LANES))
        else:
            factor = jnp.exp2((m_old[rows, :] - peak) * exp2_scale)
            l_ref[rows, :] = l_old[rows, :] * factor + added
            acc_ref[rows, :] = acc_old[rows, :] * jnp.concatenate([factor] * (LATENT_WIDTH // LANES), axis=1)
        m_ref[rows, :] = peak
        p_ref[rows, 0:width] = powers.astype(bf16)
    add = jnp.dot(p_ref[:, 0:width], values, preferred_element_type=f32)
    if m_old is None:
        acc_ref[...] = add
    else:
        acc_ref[...] += add


def state_shapes(total):
    stat = jax.ShapeDtypeStruct((total, LANES), f32)
    return [stat, stat, jax.ShapeDtypeStruct((total, LATENT_WIDTH), f32)]


def collect_suffix(key_ref, came, orders, page_width, share):
    core, member = lax.axis_index("tp"), lax.axis_index("dp") % TEAM
    half = came[0].shape[0] // 2
    for b in range(TEAM):
        rows = slice((b % 2) * half, (b % 2) * half + share)
        mine, theirs = came[b // 2][rows, page_width:], came[4 + b // 2][rows, page_width:]
        for side in range(2):
            piece = jnp.where(core == side, mine, theirs)
            source = member ^ sum(orders[side][k] for k in range(3) if (b >> k) & 1)
            at = pl.ds(pl.multiple_of(source * share, share), share)
            if side == 0:
                key_ref[at, 0:SUFFIX_LANES] = piece
            else:
                key_ref[at, SUFFIX_LANES:PADDED] = piece[:, 0 : PADDED - SUFFIX_LANES]


def attend(state, qe, qo, parts, page_width, row_block, suffix_len, tokens, suffix=None, last=None):
    n = len(parts)
    total = qe.shape[0]
    first = state is None
    per = page_width // WIDTH
    pieces = []
    for k, (page, _, _) in enumerate(parts):
        step = min(page.shape[0], CHUNK // 2)
        pieces += [(k, at, step) for at in range(0, page.shape[0], step)]
    groups, size = [[]], 0
    for piece in pieces:
        if size + piece[2] > CHUNK:
            groups.append([])
            size = 0
        groups[-1].append(piece)
        size += piece[2]
    widest = max(sum(p[2] for p in g) for g in groups) * per + (tokens if suffix else 0)
    n_came = 8 if suffix else 0

    def body(len_ref, qe_ref, qo_ref, *refs):
        page_refs, bias_refs, refs = refs[:n], refs[n : 2 * n], refs[2 * n :]
        came, refs = refs[:n_came], refs[n_came:]
        old = (None, None, None)
        if not first:
            old, refs = tuple(refs[:3]), refs[3:]
        if last:
            out_ref, refs = refs[0], refs[1:]
        new = tuple(refs[:3])
        s_ref, p_ref = refs[3:5]
        length = len_ref[lax.axis_index("dp") // TEAM]
        for number, group in enumerate(groups):
            evens, odds, ropes, even_bias, odd_bias = [], [], [], [], []
            for k, at, step in group:
                even, odd, rope = stack_keys(page_refs[k], slice(at, at + step), page_width)
                evens.append(even)
                odds.append(odd)
                ropes.append(rope)
                row, half_keys = parts[k][2], step * per // 2
                even_bias.append(bias_refs[k][row : row + 1, at * per : at * per + half_keys])
                odd_bias.append(bias_refs[k][row : row + 1, at * per + half_keys : at * per + 2 * half_keys])
            rope = jnp.concatenate(ropes, axis=0)
            even, odd = jnp.concatenate(evens, axis=0), jnp.concatenate(odds, axis=0)
            width = even.shape[0]
            s_ref[:, 0:width] = dot_nt(qe_ref[...], jnp.concatenate([even, rope], axis=1))
            s_ref[:, width : 2 * width] = dot_nt(qo_ref[...], jnp.concatenate([odd, rope], axis=1))
            width *= 2
            values, causal = [even, odd], None
            if suffix and number == len(groups) - 1:
                key_ref = refs[5]
                collect_suffix(key_ref, came, suffix[1], page_width, tokens // TEAM)
                s_ref[:, width : width + tokens] = dot_nt(qe_ref[...], key_ref[...])
                width += tokens
                values.append(key_ref[:, 0:LATENT_WIDTH])

                def causal(r, count):
                    u = iota((count, tokens), 1)
                    t = (iota((count, tokens), 0) + r) % tokens
                    return jnp.where((u <= t) & (u < length), 0.0, masked_score)

            bias = jnp.concatenate(even_bias + odd_bias, axis=1)
            softmax_step(s_ref, p_ref, width, bias, causal, old, new, jnp.concatenate(values, axis=0), row_block)
            old = new
        if last:
            _, l_ref, acc_ref = new
            live = iota((tokens, LATENT_WIDTH), 0) < length
            for h in range(last):
                rows = slice(h * tokens, (h + 1) * tokens)
                share = 1.0 / l_ref[rows, :]
                out = acc_ref[rows, :] * jnp.concatenate([share] * (LATENT_WIDTH // LANES), axis=1)
                out_ref[:, h * LATENT_WIDTH : (h + 1) * LATENT_WIDTH] = jnp.where(live, out, 0.0).astype(bf16)

    pages = [p for p, _, _ in parts]
    biases = [b for _, b, _ in parts]
    came = list(suffix[0]) if suffix else []
    carried = [] if first else list(state)
    n_in = 2 + 2 * n + len(came) + len(carried)
    scratch = [pltpu.VMEM((total, widest), f32), pltpu.VMEM((total, widest), bf16)]
    if suffix:
        scratch.append(pltpu.VMEM((tokens, PADDED), bf16))
    mib = 9 + (sum(p.size * 2 for p in pages + came) >> 20)
    outs = state_shapes(total)
    if last:
        scratch = [pltpu.VMEM(x.shape, f32) for x in outs] + scratch
        outs = [jax.ShapeDtypeStruct((tokens, last * LATENT_WIDTH), bf16)]
    return call(body, 1, n_in, outs, mib, scratch_shapes=scratch)(suffix_len, qe, qo, *pages, *biases, *came, *carried)


def program(pool, page_holder, page_slot, suffix_latent_rows, prefill_queries, suffix_len, decode_queries, decode_len):
    ranks = lax.axis_size("dp")
    teams = ranks // TEAM
    pull = page_holder.shape[0]
    cap = (pull + ranks - 1) // ranks
    width = -(-ranks * cap // LANES) * LANES
    page_width = pool.shape[1]
    tokens = prefill_queries.shape[1]
    heads = prefill_queries.shape[2] // WIDTH
    share = suffix_latent_rows.shape[1] // WIDTH

    table = request_table(jnp.stack([page_holder, page_slot]), ranks, cap, width)
    block = TEAM * cap
    split = block % 32 == 0
    if split:
        streams = [(j, block // 2) for j in range(teams)]
    else:
        streams = [(0, teams * block // 2)]
    suffix = jnp.pad(suffix_latent_rows.reshape(share, WIDTH), ((0, 0), (0, 2 * SUFFIX_LANES - WIDTH)))
    pool = pair_pool(pool)
    sent = []
    step = 1
    while step < ranks:
        table = table + xperm(table, (step, step))
        step *= 2
        if step == TEAM and split:
            sent += gather_pages(table, pool, suffix, streams[:1], cap)
    if split:
        sent += gather_pages(table, pool, None, streams[1:], cap)
    else:
        sent += gather_pages(table, pool, suffix, streams, cap)
    qe, qo = prepare(prefill_queries[0], heads)
    dq = decode_queries.reshape(decode_queries.shape[0], -1, WIDTH)
    decode_part = decode(decode_len, pool, dq)

    orders = [((1, 2, 4), (2, 4, 1)), ((4, 2, 1), (1, 4, 2))]
    orders = [orders[n % 2] for n in range(len(streams))]
    masks_of = key_masks(table, streams, cap, orders, page_width // WIDTH)

    came = []
    for n, (base, half) in enumerate(streams):
        rows = sent[n]
        unit = min(block, half)
        pieces = []
        for at in range(0, half, unit):
            masks = tuple(TEAM * (base + (c * half + at) // block) for c in range(2))
            piece = rows[at : at + unit, :page_width] if half > unit else rows
            pieces.append(xperm(piece, masks) if any(masks) else piece)
        if half > unit:
            rows = jnp.concatenate([jnp.concatenate(pieces, axis=0), rows[:, page_width:]], axis=1)
        else:
            rows = pieces[0]
        masks = list(zip(*orders[n]))
        got = xperm(rows, masks[0])
        both = jnp.concatenate([rows, got], axis=0)
        second = xperm(both, masks[1])
        third = xperm(both, masks[2])
        fourth = xperm(second, masks[2])
        own = [both, second, third, fourth]
        other = []
        for piece in own:
            other.append(sibling(piece))
        came.append((own, other))

    row_block = 128
    plan = []
    for n in range(len(streams)):
        own, other = came[n]
        piece = [[(own[k], masks_of[n], k), (other[k], masks_of[n], 4 + k)] for k in range(4)]
        plan.append((f"att{n}a", piece[0] + piece[1]))
        if n < len(streams) - 1:
            plan.append((f"att{n}b", piece[2] + piece[3]))
        else:
            plan.append((f"att{n}b", piece[2]))
            plan.append((f"att{n}c", piece[3]))
    tail = "att0b" if len(streams) > 1 else plan[-1][0]
    state = None
    for n, (name, group) in enumerate(plan):
        suffix = (came[0][0] + came[0][1], orders[0]) if name == tail else None
        last = heads if n == len(plan) - 1 else None
        state = attend(state, qe, qo, group, page_width, row_block, suffix_len, tokens, suffix, last)
    return (state[None], decode_part)


def solution(mesh):
    placed = (
        P(("groups", "dp"), None),
        P(("groups", "dp")),
        P(("groups", "dp")),
        P(("groups", "dp"), None),
        P(("groups", "dp"), None, "tp"),
        P("groups"),
        P(("groups", "dp"), "tp"),
        P(("groups", "dp")),
    )
    return jax.shard_map(
        program,
        mesh=mesh,
        in_specs=placed,
        out_specs=(P(("groups", "dp"), None, "tp"), P(("groups", "dp"), "tp")),
        check_vma=False,
    )
```

```python
import math

import jax
import jax.numpy as jnp
from jax import lax
from jax.experimental import pallas as pl
from jax.experimental.pallas import tpu as pltpu
from jax.sharding import PartitionSpec as P


LATENT_WIDTH = 512
ROTARY_WIDTH = 64
WIDTH = LATENT_WIDTH + ROTARY_WIDTH
PADDED = 640
PAIR = 2 * WIDTH
TEAM = 8
LANES = 128
SUFFIX_LANES = 384
CHUNK = 128

softmax_scale = 192.0 ** (-0.5)
exp2_scale = softmax_scale * math.log2(math.e)
masked_score = -1e30


f32 = jnp.float32
bf16 = jnp.bfloat16


def iota(shape, dim):
    return lax.broadcasted_iota(jnp.int32, shape, dim)


def vmem():
    return pl.BlockSpec(memory_space=pltpu.VMEM)


def smem():
    return pl.BlockSpec(memory_space=pltpu.SMEM)


def call(body, n_smem, n_in, outs, mib=12, **kw):
    return pl.pallas_call(
        body,
        in_specs=[smem()] * n_smem + [vmem()] * n_in,
        out_specs=tuple(vmem() for _ in outs) if len(outs) > 1 else vmem(),
        out_shape=tuple(outs) if len(outs) > 1 else outs[0],
        compiler_params=pltpu.CompilerParams(vmem_limit_bytes=mib << 20),
        **kw,
    )


def xperm(value, masks):
    n, cores = lax.axis_size("dp"), lax.axis_size("tp")
    pairs = [(d * cores + c, (d ^ masks[c % 2]) * cores + c) for d in range(n) for c in range(cores)]
    return lax.ppermute(value, ("dp", "tp"), pairs)


def sibling(value):
    return lax.ppermute(value, "tp", [(0, 1), (1, 0)])


def request_table(asked, ranks, cap, width):
    count = asked.shape[1]

    def body(asked_ref, out_ref):
        hrow = jnp.broadcast_to(asked_ref[0:1, :], (count, count))
        srow = jnp.broadcast_to(asked_ref[1:2, :], (count, count))
        i, j = iota((count, count), 0), iota((count, count), 1)
        hcol = jnp.sum(jnp.where(i == j, hrow, 0), axis=1, keepdims=True)
        scol = jnp.sum(jnp.where(i == j, srow, 0), axis=1, keepdims=True)
        rank = jnp.sum(jnp.where((hrow == hcol) & (j < i), 1, 0), axis=1, keepdims=True)
        lane = hcol * cap + rank
        hit = jnp.where(iota((count, width), 1) == lane, scol + 1, 0)
        row = jnp.sum(hit, axis=0, keepdims=True)
        out_ref[...] = jnp.where(iota((ranks, width), 0) == lax.axis_index("dp"), row, 0)

    return call(body, 0, 1, [jax.ShapeDtypeStruct((ranks, width), jnp.int32)], 4)(asked)


def paired(page, page_width):
    out = []
    for b in range(0, page_width, PAIR):
        out.append(page[:, b : b + 512])
        out.append(page[:, b + 576 : b + 1088])
        out.append(jnp.concatenate([page[:, b + 512 : b + 576], page[:, b + 1088 : b + 1152]], axis=1))
    return jnp.concatenate(out, axis=1)


def prepare(queries, heads):
    tokens = queries.shape[0]

    def body(q_ref, qe_out, qo_out):
        zero = jnp.zeros((tokens, ROTARY_WIDTH), bf16)
        for h in range(heads):
            b = h * WIDTH
            nope = q_ref[:, b : b + 512]
            rope = q_ref[:, b + 512 : b + 576]
            rows = slice(h * tokens, (h + 1) * tokens)
            qe_out[rows, 0:512] = nope
            qo_out[rows, 0:512] = nope
            qe_out[rows, 512:640] = jnp.concatenate([rope, zero], axis=1)
            qo_out[rows, 512:640] = jnp.concatenate([zero, rope], axis=1)

    q_shape = jax.ShapeDtypeStruct((heads * tokens, PADDED), bf16)
    return call(body, 0, 1, [q_shape, q_shape])(queries)


def pair_pool(pool):
    def body(pool_ref, out_ref):
        out_ref[...] = paired(pool_ref[...], pool_ref.shape[1])

    return call(body, 0, 1, [jax.ShapeDtypeStruct(pool.shape, bf16)])(pool)


def stack_keys(page_ref, rows, page_width):
    pairs = page_width // PAIR
    even = jnp.concatenate([page_ref[rows, j * PAIR : j * PAIR + 512] for j in range(pairs)], axis=0)
    odd = jnp.concatenate([page_ref[rows, j * PAIR + 512 : j * PAIR + 1024] for j in range(pairs)], axis=0)
    rope = jnp.concatenate([page_ref[rows, j * PAIR + 1024 : j * PAIR + 1152] for j in range(pairs)], axis=0)
    return even, odd, rope


def dot_nt(a, b):
    return lax.dot_general(a, b, (((1,), (1,)), ((), ())), preferred_element_type=f32)


def decode(lens, pool, qe, begin, end, before=None):
    rows, heads, _ = qe.shape
    pages, page_width = pool.shape
    per_row = pages // rows
    pairs = page_width // PAIR

    def body(len_ref, pool_ref, q_ref, *refs):
        out_ref = refs[-1]
        key_rows = pairs * per_row
        s = iota((heads, key_rows), 1)
        pos = (s % per_row) * (2 * pairs) + 2 * (s // per_row)
        zero = jnp.zeros((heads, ROTARY_WIDTH), bf16)
        done = [] if before is None else [refs[0][...]]
        for g in range(begin, end):
            even, odd, rope = stack_keys(pool_ref, slice(g * per_row, (g + 1) * per_row), page_width)
            nope_q = q_ref[g, :, 0:512]
            rope_q = q_ref[g, :, 512:576]
            re = jnp.concatenate([rope_q, zero], axis=1)
            ro = jnp.concatenate([zero, rope_q], axis=1)
            se = dot_nt(nope_q, even) + dot_nt(re, rope)
            so = dot_nt(nope_q, odd) + dot_nt(ro, rope)
            se = jnp.where(pos < len_ref[g], se, masked_score)
            so = jnp.where(pos + 1 < len_ref[g], so, masked_score)
            peak = jnp.maximum(jnp.max(se, axis=1, keepdims=True), jnp.max(so, axis=1, keepdims=True))
            pe = jnp.exp2((se - peak) * exp2_scale)
            po = jnp.exp2((so - peak) * exp2_scale)
            den = jnp.sum(pe, axis=1, keepdims=True) + jnp.sum(po, axis=1, keepdims=True)
            out = jnp.dot(pe.astype(bf16), even, preferred_element_type=f32)
            out += jnp.dot(po.astype(bf16), odd, preferred_element_type=f32)
            done.append((out / den).astype(bf16))
        done = jnp.concatenate(done, axis=0)
        if before is None:
            out_ref[...] = done
            return
        i, j = iota((rows * heads, rows * heads), 0), iota((rows * heads, rows * heads), 1)
        swap = jnp.where(j == (i % rows) * heads + i // rows, 1.0, 0.0).astype(bf16)
        done = jnp.dot(swap, done, preferred_element_type=f32)
        for h in range(heads):
            out_ref[:, h * LATENT_WIDTH : (h + 1) * LATENT_WIDTH] = done[h * rows : (h + 1) * rows, :].astype(bf16)

    if before is None:
        out = jax.ShapeDtypeStruct(((end - begin) * heads, LATENT_WIDTH), bf16)
        return call(body, 1, 2, [out])(lens, pool, qe)
    out = jax.ShapeDtypeStruct((rows, heads * LATENT_WIDTH), bf16)
    return call(body, 1, 3, [out])(lens, pool, qe, before)


def gather_pages(table, pool, suffix, streams, cap):
    ranks, width = table.shape
    pages, page_width = pool.shape
    block = TEAM * cap
    total = sum(half for _, half in streams)

    def body(table_ref, pool_ref, *outs):
        if suffix is not None:
            suffix_ref, outs = outs[0], outs[1:]
        me, core = lax.axis_index("dp"), lax.axis_index("tp")
        team = me // TEAM
        tab = table_ref[...].astype(f32).astype(bf16)

        def position(shape):
            n = iota(shape, 0)
            g = jnp.zeros(shape, jnp.int32)
            base = jnp.zeros(shape, jnp.int32)
            at = 0
            for first, half in streams:
                inside = (n >= at) & (n < at + half)
                g = jnp.where(inside, n - at + core * half, g)
                base = jnp.where(inside, first, base)
                at += half
            return base, g

        base, g = position((total, ranks))
        source = (team ^ (base + g // block)) * TEAM + (g % block) // cap
        pick = jnp.where(iota((total, ranks), 1) == source, 1.0, 0.0).astype(bf16)
        spread = jnp.dot(pick, tab, preferred_element_type=f32)
        _, g = position((total, width))
        mine = iota((total, width), 1) == me * cap + g % cap
        slot = jnp.sum(jnp.where(mine, spread, 0.0), axis=1, keepdims=True)
        hot = jnp.where(iota((total, pages), 1) + 1 == slot.astype(jnp.int32), 1.0, 0.0).astype(bf16)
        rows = jnp.dot(hot, pool_ref[...], preferred_element_type=f32).astype(bf16)
        at = 0
        for n, (_, half) in enumerate(streams):
            outs[n][:, 0:page_width] = rows[at : at + half]
            at += half
            if suffix is not None and n == 0:
                left = suffix_ref[:, 0:SUFFIX_LANES]
                right = suffix_ref[:, SUFFIX_LANES : 2 * SUFFIX_LANES]
                if half > left.shape[0]:
                    outs[n][:, page_width:] = jnp.zeros((half, SUFFIX_LANES), bf16)
                outs[n][0 : left.shape[0], page_width:] = jnp.where(core == 0, left, right)

    outs = [
        jax.ShapeDtypeStruct((half, page_width + (SUFFIX_LANES if n == 0 and suffix is not None else 0)), bf16)
        for n, (_, half) in enumerate(streams)
    ]
    given = [table, pool] + ([] if suffix is None else [suffix])
    out = call(body, 0, len(given), outs)(*given)
    return out if len(outs) > 1 else (out,)


def key_masks(table, streams, cap, orders, tokens):
    ranks, width = table.shape
    block = TEAM * cap

    def body(table_ref, *outs):
        me, core = lax.axis_index("dp"), lax.axis_index("tp")
        team, member = me // TEAM, me % TEAM
        tab = table_ref[...].astype(f32).astype(bf16)
        for n, (base, half) in enumerate(streams):
            total = TEAM * half
            for side in range(2):
                owner = (core + side) % 2
                p = iota((width, total), 1)
                b, i = p // half, p % half
                away = jnp.zeros((width, total), jnp.int32)
                for k in range(3):
                    step = jnp.where(owner == 0, orders[n][0][k], orders[n][1][k])
                    away += ((b // (1 << k)) % 2) * step
                g = owner * half + i
                holder = (team ^ (base + g // block)) * TEAM + (member ^ away)
                sel = jnp.where(iota((width, total), 0) == holder * cap + g % cap, 1.0, 0.0).astype(bf16)
                q = iota((ranks, total), 1)
                asker = team * TEAM + ((owner * half + q % half) % block) // cap
                found = jnp.dot(tab, sel, preferred_element_type=f32)
                found = jnp.sum(jnp.where(iota((ranks, total), 0) == asker, found, 0.0), axis=0, keepdims=True)
                found = jnp.where(found > 0.0, 0.0, masked_score)
                for k in range(4):
                    wide = []
                    for at in range(k * 2 * half, (k + 1) * 2 * half, min(2 * half, CHUNK // 2)):
                        wide += [found[:, at : at + min(2 * half, CHUNK // 2)]] * tokens
                    outs[n][side * 4 + k : side * 4 + k + 1, :] = jnp.concatenate(wide, axis=1)

    outs = [jax.ShapeDtypeStruct((8, 2 * half * tokens), f32) for _, half in streams]
    out = call(body, 0, 1, outs)(table)
    return out if len(outs) > 1 else (out,)


def softmax_step(s_ref, p_ref, width, bias, causal, old_state, new_state, values, row_block):
    m_old, l_old, acc_old = old_state
    m_ref, l_ref, acc_ref = new_state
    total = s_ref.shape[0]
    for r in range(0, total, row_block):
        rows = slice(r, r + row_block)
        if causal is None:
            scores = s_ref[rows, 0:width] + bias
        else:
            plain = bias.shape[1]
            scores = jnp.concatenate([s_ref[rows, 0:plain] + bias, s_ref[rows, plain:width] + causal(r, row_block)], axis=1)
        peak = jnp.max(scores, axis=1, keepdims=True)
        if m_old is None:
            peak = jnp.broadcast_to(peak, (row_block, LANES))
        else:
            peak = jnp.maximum(m_old[rows, :], peak)
        powers = jnp.exp2((scores - jnp.concatenate([peak] * (width // LANES), axis=1)) * exp2_scale)
        added = jnp.sum(powers, axis=1, keepdims=True)
        if m_old is None:
            l_ref[rows, :] = jnp.broadcast_to(added, (row_block, LANES))
        else:
            factor = jnp.exp2((m_old[rows, :] - peak) * exp2_scale)
            l_ref[rows, :] = l_old[rows, :] * factor + added
            acc_ref[rows, :] = acc_old[rows, :] * jnp.concatenate([factor] * (LATENT_WIDTH // LANES), axis=1)
        m_ref[rows, :] = peak
        p_ref[rows, 0:width] = powers.astype(bf16)
    add = jnp.dot(p_ref[:, 0:width], values, preferred_element_type=f32)
    if m_old is None:
        acc_ref[...] = add
    else:
        acc_ref[...] += add


def state_shapes(total):
    stat = jax.ShapeDtypeStruct((total, LANES), f32)
    return [stat, stat, jax.ShapeDtypeStruct((total, LATENT_WIDTH), f32)]


def collect_suffix(key_ref, came, orders, page_width, share):
    core, member = lax.axis_index("tp"), lax.axis_index("dp") % TEAM
    half = came[0].shape[0] // 2
    for b in range(TEAM):
        rows = slice((b % 2) * half, (b % 2) * half + share)
        mine, theirs = came[b // 2][rows, page_width:], came[4 + b // 2][rows, page_width:]
        for side in range(2):
            piece = jnp.where(core == side, mine, theirs)
            source = member ^ sum(orders[side][k] for k in range(3) if (b >> k) & 1)
            at = pl.ds(pl.multiple_of(source * share, share), share)
            if side == 0:
                key_ref[at, 0:SUFFIX_LANES] = piece
            else:
                key_ref[at, SUFFIX_LANES:PADDED] = piece[:, 0 : PADDED - SUFFIX_LANES]


def attend(state, qe, qo, parts, page_width, row_block, suffix_len, tokens, suffix=None, last=None):
    n = len(parts)
    total = qe.shape[0]
    first = state is None
    per = page_width // WIDTH
    pieces = []
    for k, (page, _, _) in enumerate(parts):
        step = min(page.shape[0], CHUNK // 2)
        pieces += [(k, at, step) for at in range(0, page.shape[0], step)]
    groups, size = [[]], 0
    for piece in pieces:
        if size + piece[2] > CHUNK:
            groups.append([])
            size = 0
        groups[-1].append(piece)
        size += piece[2]
    widest = max(sum(p[2] for p in g) for g in groups) * per + (tokens if suffix else 0)
    n_came = 8 if suffix else 0

    def body(len_ref, qe_ref, qo_ref, *refs):
        page_refs, bias_refs, refs = refs[:n], refs[n : 2 * n], refs[2 * n :]
        came, refs = refs[:n_came], refs[n_came:]
        old = (None, None, None)
        if not first:
            old, refs = tuple(refs[:3]), refs[3:]
        if last:
            out_ref, refs = refs[0], refs[1:]
        new = tuple(refs[:3])
        s_ref, p_ref = refs[3:5]
        length = len_ref[lax.axis_index("dp") // TEAM]
        for number, group in enumerate(groups):
            evens, odds, ropes, even_bias, odd_bias = [], [], [], [], []
            for k, at, step in group:
                even, odd, rope = stack_keys(page_refs[k], slice(at, at + step), page_width)
                evens.append(even)
                odds.append(odd)
                ropes.append(rope)
                row, half_keys = parts[k][2], step * per // 2
                even_bias.append(bias_refs[k][row : row + 1, at * per : at * per + half_keys])
                odd_bias.append(bias_refs[k][row : row + 1, at * per + half_keys : at * per + 2 * half_keys])
            rope = jnp.concatenate(ropes, axis=0)
            even, odd = jnp.concatenate(evens, axis=0), jnp.concatenate(odds, axis=0)
            width = even.shape[0]
            s_ref[:, 0:width] = dot_nt(qe_ref[...], jnp.concatenate([even, rope], axis=1))
            s_ref[:, width : 2 * width] = dot_nt(qo_ref[...], jnp.concatenate([odd, rope], axis=1))
            width *= 2
            values, causal = [even, odd], None
            if suffix and number == len(groups) - 1:
                key_ref = refs[5]
                collect_suffix(key_ref, came, suffix[1], page_width, tokens // TEAM)
                s_ref[:, width : width + tokens] = dot_nt(qe_ref[...], key_ref[...])
                width += tokens
                values.append(key_ref[:, 0:LATENT_WIDTH])

                def causal(r, count):
                    u = iota((count, tokens), 1)
                    t = (iota((count, tokens), 0) + r) % tokens
                    return jnp.where((u <= t) & (u < length), 0.0, masked_score)

            bias = jnp.concatenate(even_bias + odd_bias, axis=1)
            softmax_step(s_ref, p_ref, width, bias, causal, old, new, jnp.concatenate(values, axis=0), row_block)
            old = new
        if last:
            _, l_ref, acc_ref = new
            live = iota((tokens, LATENT_WIDTH), 0) < length
            for h in range(last):
                rows = slice(h * tokens, (h + 1) * tokens)
                share = 1.0 / l_ref[rows, :]
                out = acc_ref[rows, :] * jnp.concatenate([share] * (LATENT_WIDTH // LANES), axis=1)
                out_ref[:, h * LATENT_WIDTH : (h + 1) * LATENT_WIDTH] = jnp.where(live, out, 0.0).astype(bf16)

    pages = [p for p, _, _ in parts]
    biases = [b for _, b, _ in parts]
    came = list(suffix[0]) if suffix else []
    carried = [] if first else list(state)
    n_in = 2 + 2 * n + len(came) + len(carried)
    scratch = [pltpu.VMEM((total, widest), f32), pltpu.VMEM((total, widest), bf16)]
    if suffix:
        scratch.append(pltpu.VMEM((tokens, PADDED), bf16))
    mib = 9 + (sum(p.size * 2 for p in pages + came) >> 20)
    outs = state_shapes(total)
    if last:
        scratch = [pltpu.VMEM(x.shape, f32) for x in outs] + scratch
        outs = [jax.ShapeDtypeStruct((tokens, last * LATENT_WIDTH), bf16)]
    return call(body, 1, n_in, outs, mib, scratch_shapes=scratch)(suffix_len, qe, qo, *pages, *biases, *came, *carried)


def program(pool, page_holder, page_slot, suffix_latent_rows, prefill_queries, suffix_len, decode_queries, decode_len):
    ranks = lax.axis_size("dp")
    teams = ranks // TEAM
    pull = page_holder.shape[0]
    cap = (pull + ranks - 1) // ranks
    width = -(-ranks * cap // LANES) * LANES
    page_width = pool.shape[1]
    tokens = prefill_queries.shape[1]
    heads = prefill_queries.shape[2] // WIDTH
    share = suffix_latent_rows.shape[1] // WIDTH

    table = request_table(jnp.stack([page_holder, page_slot]), ranks, cap, width)
    block = TEAM * cap
    split = block % 32 == 0
    if split:
        streams = [(j, block // 2) for j in range(teams)]
    else:
        streams = [(0, teams * block // 2)]
    suffix = jnp.pad(suffix_latent_rows.reshape(share, WIDTH), ((0, 0), (0, 2 * SUFFIX_LANES - WIDTH)))
    pool = pair_pool(pool)
    sent = []
    step = 1
    while step < ranks:
        table = table + xperm(table, (step, step))
        step *= 2
        if step == TEAM and split:
            sent += gather_pages(table, pool, suffix, streams[:1], cap)
    if split:
        sent += gather_pages(table, pool, None, streams[1:], cap)
    else:
        sent += gather_pages(table, pool, suffix, streams, cap)
    qe, qo = prepare(prefill_queries[0], heads)
    dq = decode_queries.reshape(decode_queries.shape[0], -1, WIDTH)
    middle = dq.shape[0] // 2
    some = decode(decode_len, pool, dq, 0, middle)
    decode_part = decode(decode_len, pool, dq, middle, dq.shape[0], some)

    orders = [((1, 2, 4), (2, 4, 1)), ((4, 2, 1), (1, 4, 2))]
    orders = [orders[n % 2] for n in range(len(streams))]
    masks_of = key_masks(table, streams, cap, orders, page_width // WIDTH)

    came = []
    for n, (base, half) in enumerate(streams):
        rows = sent[n]
        unit = min(block, half)
        pieces = []
        for at in range(0, half, unit):
            masks = tuple(TEAM * (base + (c * half + at) // block) for c in range(2))
            piece = rows[at : at + unit, :page_width] if half > unit else rows
            pieces.append(xperm(piece, masks) if any(masks) else piece)
        if half > unit:
            rows = jnp.concatenate([jnp.concatenate(pieces, axis=0), rows[:, page_width:]], axis=1)
        else:
            rows = pieces[0]
        masks = list(zip(*orders[n]))
        got = xperm(rows, masks[0])
        both = jnp.concatenate([rows, got], axis=0)
        second = xperm(both, masks[1])
        third = xperm(both, masks[2])
        fourth = xperm(second, masks[2])
        own = [both, second, third, fourth]
        other = []
        for piece in own:
            other.append(sibling(piece))
        came.append((own, other))

    row_block = 128
    pieces = []
    for n in range(len(streams)):
        own, other = came[n]
        pieces.append([[(own[k], masks_of[n], k), (other[k], masks_of[n], 4 + k)] for k in range(4)])
    plan = [("att0a", pieces[0][0] + pieces[0][1])]
    if len(streams) > 1:
        plan += [("att1a", pieces[1][0]), ("att0b", pieces[0][2] + pieces[0][3])]
        for n in range(1, len(streams)):
            if n > 1:
                plan.append((f"att{n}a", pieces[n][0]))
            plan += [(f"att{n}b", pieces[n][1] + pieces[n][2]), (f"att{n}c", pieces[n][3])]
    else:
        plan += [("att0b", pieces[0][2]), ("att0c", pieces[0][3])]
    tail = "att0b" if len(streams) > 1 else plan[-1][0]
    state = None
    for n, (name, group) in enumerate(plan):
        suffix = (came[0][0] + came[0][1], orders[0]) if name == tail else None
        last = heads if n == len(plan) - 1 else None
        state = attend(state, qe, qo, group, page_width, row_block, suffix_len, tokens, suffix, last)
    return (state[None], decode_part)


def solution(mesh):
    placed = (
        P(("groups", "dp"), None),
        P(("groups", "dp")),
        P(("groups", "dp")),
        P(("groups", "dp"), None),
        P(("groups", "dp"), None, "tp"),
        P("groups"),
        P(("groups", "dp"), "tp"),
        P(("groups", "dp")),
    )
    return jax.shard_map(
        program,
        mesh=mesh,
        in_specs=placed,
        out_specs=(P(("groups", "dp"), None, "tp"), P(("groups", "dp"), "tp")),
        check_vma=False,
    )
```

```python
import math

import jax
import jax.numpy as jnp
from jax import lax
from jax.experimental import pallas as pl
from jax.experimental.pallas import tpu as pltpu
from jax.sharding import PartitionSpec as P


LATENT_WIDTH = 512
ROTARY_WIDTH = 64
WIDTH = LATENT_WIDTH + ROTARY_WIDTH
PADDED = 640
PAIR = 2 * WIDTH
TEAM = 8
LANES = 128
SUFFIX_LANES = 384
CHUNK = 128

softmax_scale = 192.0 ** (-0.5)
exp2_scale = softmax_scale * math.log2(math.e)
masked_score = -1e30


f32 = jnp.float32
bf16 = jnp.bfloat16


def iota(shape, dim):
    return lax.broadcasted_iota(jnp.int32, shape, dim)


def vmem():
    return pl.BlockSpec(memory_space=pltpu.VMEM)


def smem():
    return pl.BlockSpec(memory_space=pltpu.SMEM)


def call(body, n_smem, n_in, outs, mib=12, **kw):
    return pl.pallas_call(
        body,
        in_specs=[smem()] * n_smem + [vmem()] * n_in,
        out_specs=tuple(vmem() for _ in outs) if len(outs) > 1 else vmem(),
        out_shape=tuple(outs) if len(outs) > 1 else outs[0],
        compiler_params=pltpu.CompilerParams(vmem_limit_bytes=mib << 20),
        **kw,
    )


def xperm(value, masks, flip=0):
    n, cores = lax.axis_size("dp"), lax.axis_size("tp")
    pairs = [(d * cores + c, (d ^ masks[c]) * cores + (c ^ flip)) for d in range(n) for c in range(cores)]
    return lax.ppermute(value, ("dp", "tp"), pairs)


def sibling(value):
    return lax.ppermute(value, "tp", [(0, 1), (1, 0)])


def request_table(asked, ranks, cap, width):
    count = asked.shape[1]

    def body(asked_ref, out_ref):
        hrow = jnp.broadcast_to(asked_ref[0:1, :], (count, count))
        srow = jnp.broadcast_to(asked_ref[1:2, :], (count, count))
        i, j = iota((count, count), 0), iota((count, count), 1)
        hcol = jnp.sum(jnp.where(i == j, hrow, 0), axis=1, keepdims=True)
        scol = jnp.sum(jnp.where(i == j, srow, 0), axis=1, keepdims=True)
        rank = jnp.sum(jnp.where((hrow == hcol) & (j < i), 1, 0), axis=1, keepdims=True)
        lane = hcol * cap + rank
        hit = jnp.where(iota((count, width), 1) == lane, scol + 1, 0)
        row = jnp.sum(hit, axis=0, keepdims=True)
        out_ref[...] = jnp.where(iota((ranks, width), 0) == lax.axis_index("dp"), row, 0)

    return call(body, 0, 1, [jax.ShapeDtypeStruct((ranks, width), jnp.int32)], 4)(asked)


def paired(page, page_width):
    out = []
    for b in range(0, page_width, PAIR):
        out.append(page[:, b : b + 512])
        out.append(page[:, b + 576 : b + 1088])
        out.append(jnp.concatenate([page[:, b + 512 : b + 576], page[:, b + 1088 : b + 1152]], axis=1))
    return jnp.concatenate(out, axis=1)


def prepare(queries, heads):
    tokens = queries.shape[0]

    def body(q_ref, qe_out, qo_out):
        zero = jnp.zeros((tokens, ROTARY_WIDTH), bf16)
        for h in range(heads):
            b = h * WIDTH
            nope = q_ref[:, b : b + 512]
            rope = q_ref[:, b + 512 : b + 576]
            rows = slice(h * tokens, (h + 1) * tokens)
            qe_out[rows, 0:512] = nope
            qo_out[rows, 0:512] = nope
            qe_out[rows, 512:640] = jnp.concatenate([rope, zero], axis=1)
            qo_out[rows, 512:640] = jnp.concatenate([zero, rope], axis=1)

    q_shape = jax.ShapeDtypeStruct((heads * tokens, PADDED), bf16)
    return call(body, 0, 1, [q_shape, q_shape])(queries)


def pair_pool(pool):
    def body(pool_ref, out_ref):
        out_ref[...] = paired(pool_ref[...], pool_ref.shape[1])

    return call(body, 0, 1, [jax.ShapeDtypeStruct(pool.shape, bf16)])(pool)


def stack_keys(page_ref, rows, page_width):
    pairs = page_width // PAIR
    even = jnp.concatenate([page_ref[rows, j * PAIR : j * PAIR + 512] for j in range(pairs)], axis=0)
    odd = jnp.concatenate([page_ref[rows, j * PAIR + 512 : j * PAIR + 1024] for j in range(pairs)], axis=0)
    rope = jnp.concatenate([page_ref[rows, j * PAIR + 1024 : j * PAIR + 1152] for j in range(pairs)], axis=0)
    return even, odd, rope


def dot_nt(a, b):
    return lax.dot_general(a, b, (((1,), (1,)), ((), ())), preferred_element_type=f32)


def decode(lens, pool, qe, begin, end, before=None):
    rows, heads, _ = qe.shape
    pages, page_width = pool.shape
    per_row = pages // rows
    pairs = page_width // PAIR

    def body(len_ref, pool_ref, q_ref, *refs):
        out_ref = refs[-1]
        key_rows = pairs * per_row
        s = iota((heads, key_rows), 1)
        pos = (s % per_row) * (2 * pairs) + 2 * (s // per_row)
        zero = jnp.zeros((heads, ROTARY_WIDTH), bf16)
        done = [] if before is None else [refs[0][...]]
        for g in range(begin, end):
            even, odd, rope = stack_keys(pool_ref, slice(g * per_row, (g + 1) * per_row), page_width)
            nope_q = q_ref[g, :, 0:512]
            rope_q = q_ref[g, :, 512:576]
            re = jnp.concatenate([rope_q, zero], axis=1)
            ro = jnp.concatenate([zero, rope_q], axis=1)
            se = dot_nt(nope_q, even) + dot_nt(re, rope)
            so = dot_nt(nope_q, odd) + dot_nt(ro, rope)
            se = jnp.where(pos < len_ref[g], se, masked_score)
            so = jnp.where(pos + 1 < len_ref[g], so, masked_score)
            peak = jnp.maximum(jnp.max(se, axis=1, keepdims=True), jnp.max(so, axis=1, keepdims=True))
            pe = jnp.exp2((se - peak) * exp2_scale)
            po = jnp.exp2((so - peak) * exp2_scale)
            den = jnp.sum(pe, axis=1, keepdims=True) + jnp.sum(po, axis=1, keepdims=True)
            out = jnp.dot(pe.astype(bf16), even, preferred_element_type=f32)
            out += jnp.dot(po.astype(bf16), odd, preferred_element_type=f32)
            done.append((out / den).astype(bf16))
        done = jnp.concatenate(done, axis=0)
        if before is None:
            out_ref[...] = done
            return
        i, j = iota((rows * heads, rows * heads), 0), iota((rows * heads, rows * heads), 1)
        swap = jnp.where(j == (i % rows) * heads + i // rows, 1.0, 0.0).astype(bf16)
        done = jnp.dot(swap, done, preferred_element_type=f32)
        for h in range(heads):
            out_ref[:, h * LATENT_WIDTH : (h + 1) * LATENT_WIDTH] = done[h * rows : (h + 1) * rows, :].astype(bf16)

    if before is None:
        out = jax.ShapeDtypeStruct(((end - begin) * heads, LATENT_WIDTH), bf16)
        return call(body, 1, 2, [out])(lens, pool, qe)
    out = jax.ShapeDtypeStruct((rows, heads * LATENT_WIDTH), bf16)
    return call(body, 1, 3, [out])(lens, pool, qe, before)


def gather_pages(table, pool, suffix, streams, cap):
    ranks, width = table.shape
    pages, page_width = pool.shape
    block = TEAM * cap
    total = sum(half for _, half in streams)

    def body(table_ref, pool_ref, *outs):
        if suffix is not None:
            suffix_ref, outs = outs[0], outs[1:]
        me, core = lax.axis_index("dp"), lax.axis_index("tp")
        team = me // TEAM
        tab = table_ref[...].astype(f32).astype(bf16)

        def position(shape):
            n = iota(shape, 0)
            g = jnp.zeros(shape, jnp.int32)
            base = jnp.zeros(shape, jnp.int32)
            at = 0
            for first, half in streams:
                inside = (n >= at) & (n < at + half)
                g = jnp.where(inside, n - at + (core if first == 0 else 1 - core) * half, g)
                base = jnp.where(inside, first, base)
                at += half
            return base, g

        base, g = position((total, ranks))
        source = (team ^ (base + g // block)) * TEAM + (g % block) // cap
        pick = jnp.where(iota((total, ranks), 1) == source, 1.0, 0.0).astype(bf16)
        spread = jnp.dot(pick, tab, preferred_element_type=f32)
        _, g = position((total, width))
        mine = iota((total, width), 1) == me * cap + g % cap
        slot = jnp.sum(jnp.where(mine, spread, 0.0), axis=1, keepdims=True)
        hot = jnp.where(iota((total, pages), 1) + 1 == slot.astype(jnp.int32), 1.0, 0.0).astype(bf16)
        rows = jnp.dot(hot, pool_ref[...], preferred_element_type=f32).astype(bf16)
        at = 0
        for n, (_, half) in enumerate(streams):
            outs[n][:, 0:page_width] = rows[at : at + half]
            at += half
            if suffix is not None and n == 0:
                left = suffix_ref[:, 0:SUFFIX_LANES]
                right = suffix_ref[:, SUFFIX_LANES : 2 * SUFFIX_LANES]
                if half > left.shape[0]:
                    outs[n][:, page_width:] = jnp.zeros((half, SUFFIX_LANES), bf16)
                outs[n][0 : left.shape[0], page_width:] = jnp.where(core == 0, left, right)

    outs = [
        jax.ShapeDtypeStruct((half, page_width + (SUFFIX_LANES if n == 0 and suffix is not None else 0)), bf16)
        for n, (_, half) in enumerate(streams)
    ]
    given = [table, pool] + ([] if suffix is None else [suffix])
    out = call(body, 0, len(given), outs)(*given)
    return out if len(outs) > 1 else (out,)


def key_masks(table, streams, cap, orders, tokens):
    ranks, width = table.shape
    block = TEAM * cap

    def body(table_ref, *outs):
        me, core = lax.axis_index("dp"), lax.axis_index("tp")
        team, member = me // TEAM, me % TEAM
        tab = table_ref[...].astype(f32).astype(bf16)
        for n, (base, half) in enumerate(streams):
            total = TEAM * half
            for side in range(2):
                p = iota((width, total), 1)
                b, i = p // half, p % half
                owner = (core + side + b // 4) % 2
                away = jnp.zeros((width, total), jnp.int32)
                for k in range(3):
                    step = jnp.where(owner == 0, orders[n][0][k], orders[n][1][k])
                    away += ((b // (1 << k)) % 2) * step
                g = owner * half + i
                holder = (team ^ (base + g // block)) * TEAM + (member ^ away)
                sel = jnp.where(iota((width, total), 0) == holder * cap + g % cap, 1.0, 0.0).astype(bf16)
                q = iota((ranks, total), 1)
                asker = team * TEAM + (((core + side + q // (4 * half)) % 2 * half + q % half) % block) // cap
                found = jnp.dot(tab, sel, preferred_element_type=f32)
                found = jnp.sum(jnp.where(iota((ranks, total), 0) == asker, found, 0.0), axis=0, keepdims=True)
                found = jnp.where(found > 0.0, 0.0, masked_score)
                for k in range(4):
                    wide = []
                    for at in range(k * 2 * half, (k + 1) * 2 * half, min(2 * half, CHUNK // 2)):
                        wide += [found[:, at : at + min(2 * half, CHUNK // 2)]] * tokens
                    outs[n][side * 4 + k : side * 4 + k + 1, :] = jnp.concatenate(wide, axis=1)

    outs = [jax.ShapeDtypeStruct((8, 2 * half * tokens), f32) for _, half in streams]
    out = call(body, 0, 1, outs)(table)
    return out if len(outs) > 1 else (out,)


def softmax_step(s_ref, p_ref, width, bias, causal, old_state, new_state, values, row_block):
    m_old, l_old, acc_old = old_state
    m_ref, l_ref, acc_ref = new_state
    total = s_ref.shape[0]
    for r in range(0, total, row_block):
        rows = slice(r, r + row_block)
        if causal is None:
            scores = s_ref[rows, 0:width] + bias
        else:
            plain = bias.shape[1]
            scores = jnp.concatenate([s_ref[rows, 0:plain] + bias, s_ref[rows, plain:width] + causal(r, row_block)], axis=1)
        peak = jnp.max(scores, axis=1, keepdims=True)
        if m_old is None:
            peak = jnp.broadcast_to(peak, (row_block, LANES))
        else:
            peak = jnp.maximum(m_old[rows, :], peak)
        powers = jnp.exp2((scores - jnp.concatenate([peak] * (width // LANES), axis=1)) * exp2_scale)
        added = jnp.sum(powers, axis=1, keepdims=True)
        if m_old is None:
            l_ref[rows, :] = jnp.broadcast_to(added, (row_block, LANES))
        else:
            factor = jnp.exp2((m_old[rows, :] - peak) * exp2_scale)
            l_ref[rows, :] = l_old[rows, :] * factor + added
            acc_ref[rows, :] = acc_old[rows, :] * jnp.concatenate([factor] * (LATENT_WIDTH // LANES), axis=1)
        m_ref[rows, :] = peak
        p_ref[rows, 0:width] = powers.astype(bf16)
    add = jnp.dot(p_ref[:, 0:width], values, preferred_element_type=f32)
    if m_old is None:
        acc_ref[...] = add
    else:
        acc_ref[...] += add


def state_shapes(total):
    stat = jax.ShapeDtypeStruct((total, LANES), f32)
    return [stat, stat, jax.ShapeDtypeStruct((total, LATENT_WIDTH), f32)]


def collect_suffix(key_ref, came, orders, page_width, share):
    core, member = lax.axis_index("tp"), lax.axis_index("dp") % TEAM
    half = came[0].shape[0] // 2
    for b in range(TEAM):
        rows = slice((b % 2) * half, (b % 2) * half + share)
        mine, theirs = came[b // 2][rows, page_width:], came[4 + b // 2][rows, page_width:]
        for side in range(2):
            piece = jnp.where(core == side ^ (b // 4), mine, theirs)
            source = member ^ sum(orders[side][k] for k in range(3) if (b >> k) & 1)
            at = pl.ds(pl.multiple_of(source * share, share), share)
            if side == 0:
                key_ref[at, 0:SUFFIX_LANES] = piece
            else:
                key_ref[at, SUFFIX_LANES:PADDED] = piece[:, 0 : PADDED - SUFFIX_LANES]


def attend(state, qe, qo, parts, page_width, row_block, suffix_len, tokens, suffix=None, last=None):
    n = len(parts)
    total = qe.shape[0]
    first = state is None
    per = page_width // WIDTH
    pieces = []
    for k, (page, _, _) in enumerate(parts):
        step = min(page.shape[0], CHUNK // 2)
        pieces += [(k, at, step) for at in range(0, page.shape[0], step)]
    groups, size = [[]], 0
    for piece in pieces:
        if size + piece[2] > CHUNK:
            groups.append([])
            size = 0
        groups[-1].append(piece)
        size += piece[2]
    widest = max(sum(p[2] for p in g) for g in groups) * per + (tokens if suffix else 0)
    n_came = 8 if suffix else 0

    def body(len_ref, qe_ref, qo_ref, *refs):
        page_refs, bias_refs, refs = refs[:n], refs[n : 2 * n], refs[2 * n :]
        came, refs = refs[:n_came], refs[n_came:]
        old = (None, None, None)
        if not first:
            old, refs = tuple(refs[:3]), refs[3:]
        if last:
            out_ref, refs = refs[0], refs[1:]
        new = tuple(refs[:3])
        s_ref, p_ref = refs[3:5]
        length = len_ref[lax.axis_index("dp") // TEAM]
        for number, group in enumerate(groups):
            evens, odds, ropes, even_bias, odd_bias = [], [], [], [], []
            for k, at, step in group:
                even, odd, rope = stack_keys(page_refs[k], slice(at, at + step), page_width)
                evens.append(even)
                odds.append(odd)
                ropes.append(rope)
                row, half_keys = parts[k][2], step * per // 2
                even_bias.append(bias_refs[k][row : row + 1, at * per : at * per + half_keys])
                odd_bias.append(bias_refs[k][row : row + 1, at * per + half_keys : at * per + 2 * half_keys])
            rope = jnp.concatenate(ropes, axis=0)
            even, odd = jnp.concatenate(evens, axis=0), jnp.concatenate(odds, axis=0)
            width = even.shape[0]
            s_ref[:, 0:width] = dot_nt(qe_ref[...], jnp.concatenate([even, rope], axis=1))
            s_ref[:, width : 2 * width] = dot_nt(qo_ref[...], jnp.concatenate([odd, rope], axis=1))
            width *= 2
            values, causal = [even, odd], None
            if suffix and number == len(groups) - 1:
                key_ref = refs[5]
                collect_suffix(key_ref, came, suffix[1], page_width, tokens // TEAM)
                s_ref[:, width : width + tokens] = dot_nt(qe_ref[...], key_ref[...])
                width += tokens
                values.append(key_ref[:, 0:LATENT_WIDTH])

                def causal(r, count):
                    u = iota((count, tokens), 1)
                    t = (iota((count, tokens), 0) + r) % tokens
                    return jnp.where((u <= t) & (u < length), 0.0, masked_score)

            bias = jnp.concatenate(even_bias + odd_bias, axis=1)
            softmax_step(s_ref, p_ref, width, bias, causal, old, new, jnp.concatenate(values, axis=0), row_block)
            old = new
        if last:
            _, l_ref, acc_ref = new
            live = iota((tokens, LATENT_WIDTH), 0) < length
            for h in range(last):
                rows = slice(h * tokens, (h + 1) * tokens)
                share = 1.0 / l_ref[rows, :]
                out = acc_ref[rows, :] * jnp.concatenate([share] * (LATENT_WIDTH // LANES), axis=1)
                out_ref[:, h * LATENT_WIDTH : (h + 1) * LATENT_WIDTH] = jnp.where(live, out, 0.0).astype(bf16)

    pages = [p for p, _, _ in parts]
    biases = [b for _, b, _ in parts]
    came = list(suffix[0]) if suffix else []
    carried = [] if first else list(state)
    n_in = 2 + 2 * n + len(came) + len(carried)
    scratch = [pltpu.VMEM((total, widest), f32), pltpu.VMEM((total, widest), bf16)]
    if suffix:
        scratch.append(pltpu.VMEM((tokens, PADDED), bf16))
    mib = 9 + (sum(p.size * 2 for p in pages + came) >> 20)
    outs = state_shapes(total)
    if last:
        scratch = [pltpu.VMEM(x.shape, f32) for x in outs] + scratch
        outs = [jax.ShapeDtypeStruct((tokens, last * LATENT_WIDTH), bf16)]
    return call(body, 1, n_in, outs, mib, scratch_shapes=scratch)(suffix_len, qe, qo, *pages, *biases, *came, *carried)


def program(pool, page_holder, page_slot, suffix_latent_rows, prefill_queries, suffix_len, decode_queries, decode_len):
    ranks = lax.axis_size("dp")
    teams = ranks // TEAM
    pull = page_holder.shape[0]
    cap = (pull + ranks - 1) // ranks
    width = -(-ranks * cap // LANES) * LANES
    page_width = pool.shape[1]
    tokens = prefill_queries.shape[1]
    heads = prefill_queries.shape[2] // WIDTH
    share = suffix_latent_rows.shape[1] // WIDTH

    table = request_table(jnp.stack([page_holder, page_slot]), ranks, cap, width)
    block = TEAM * cap
    split = block % 32 == 0
    if split:
        streams = [(j, block // 2) for j in range(teams)]
    else:
        streams = [(0, teams * block // 2)]
    suffix = jnp.pad(suffix_latent_rows.reshape(share, WIDTH), ((0, 0), (0, 2 * SUFFIX_LANES - WIDTH)))
    pool = pair_pool(pool)
    sent = []
    step = 1
    while step < ranks:
        table = table + xperm(table, (step, step), 1)
        step *= 2
        if step == TEAM and split:
            sent += gather_pages(table, pool, suffix, streams[:1], cap)
    if split:
        sent += gather_pages(table, pool, None, streams[1:], cap)
    else:
        sent += gather_pages(table, pool, suffix, streams, cap)
    qe, qo = prepare(prefill_queries[0], heads)
    dq = decode_queries.reshape(decode_queries.shape[0], -1, WIDTH)
    middle = dq.shape[0] // 2
    some = decode(decode_len, pool, dq, 0, middle)
    decode_part = decode(decode_len, pool, dq, middle, dq.shape[0], some)

    orders = [((4, 1, 2), (4, 2, 1)), ((1, 2, 4), (2, 4, 1))]
    orders = [orders[n % 2] for n in range(len(streams))]
    masks_of = key_masks(table, streams, cap, orders, page_width // WIDTH)

    came = []
    for n, (base, half) in enumerate(streams):
        rows = sent[n]
        unit = min(block, half)
        pieces = []
        for at in range(0, half, unit):
            masks = tuple(TEAM * (base + (c * half + at) // block) for c in range(2))
            piece = rows[at : at + unit, :page_width] if half > unit else rows
            pieces.append(xperm(piece, masks, int(split)) if any(masks) else piece)
        if half > unit:
            rows = jnp.concatenate([jnp.concatenate(pieces, axis=0), rows[:, page_width:]], axis=1)
        else:
            rows = pieces[0]
        masks = list(zip(*orders[n]))
        got = xperm(rows, masks[0])
        both = jnp.concatenate([rows, got], axis=0)
        second = xperm(both, masks[1])
        third = xperm(both, masks[2], 1)
        fourth = xperm(second, masks[2], 1)
        own = [both, second, third, fourth]
        other = []
        for piece in own:
            other.append(sibling(piece))
        came.append((own, other))

    row_block = 128
    pieces = []
    for n in range(len(streams)):
        own, other = came[n]
        pieces.append([[(own[k], masks_of[n], k), (other[k], masks_of[n], 4 + k)] for k in range(4)])
    plan = [("att0a", pieces[0][0] + pieces[0][1])]
    if len(streams) > 1:
        plan += [("att1a", pieces[1][0]), ("att0b", pieces[0][2] + pieces[0][3])]
        for n in range(1, len(streams)):
            if n > 1:
                plan.append((f"att{n}a", pieces[n][0]))
            plan += [(f"att{n}b", pieces[n][1] + pieces[n][2]), (f"att{n}c", pieces[n][3])]
    else:
        plan += [("att0b", pieces[0][2]), ("att0c", pieces[0][3])]
    tail = "att0b" if len(streams) > 1 else plan[-1][0]
    state = None
    for n, (name, group) in enumerate(plan):
        suffix = (came[0][0] + came[0][1], orders[0]) if name == tail else None
        last = heads if n == len(plan) - 1 else None
        state = attend(state, qe, qo, group, page_width, row_block, suffix_len, tokens, suffix, last)
    return (state[None], decode_part)


def solution(mesh):
    placed = (
        P(("groups", "dp"), None),
        P(("groups", "dp")),
        P(("groups", "dp")),
        P(("groups", "dp"), None),
        P(("groups", "dp"), None, "tp"),
        P("groups"),
        P(("groups", "dp"), "tp"),
        P(("groups", "dp")),
    )
    return jax.shard_map(
        program,
        mesh=mesh,
        in_specs=placed,
        out_specs=(P(("groups", "dp"), None, "tp"), P(("groups", "dp"), "tp")),
        check_vma=False,
    )
```

```python
import math

import jax
import jax.numpy as jnp
from jax import lax
from jax.experimental import pallas as pl
from jax.experimental.pallas import tpu as pltpu
from jax.sharding import PartitionSpec as P


LATENT_WIDTH = 512
ROTARY_WIDTH = 64
WIDTH = LATENT_WIDTH + ROTARY_WIDTH
PADDED = 640
PAIR = 2 * WIDTH
TEAM = 8
LANES = 128
SUFFIX_LANES = 384
CHUNK = 128

softmax_scale = 192.0 ** (-0.5)
exp2_scale = softmax_scale * math.log2(math.e)
masked_score = -1e30


f32 = jnp.float32
bf16 = jnp.bfloat16


def iota(shape, dim):
    return lax.broadcasted_iota(jnp.int32, shape, dim)


def vmem():
    return pl.BlockSpec(memory_space=pltpu.VMEM)


def smem():
    return pl.BlockSpec(memory_space=pltpu.SMEM)


def call(body, n_smem, n_in, outs, mib=12, **kw):
    return pl.pallas_call(
        body,
        in_specs=[smem()] * n_smem + [vmem()] * n_in,
        out_specs=tuple(vmem() for _ in outs) if len(outs) > 1 else vmem(),
        out_shape=tuple(outs) if len(outs) > 1 else outs[0],
        compiler_params=pltpu.CompilerParams(vmem_limit_bytes=mib << 20),
        **kw,
    )


def xperm(value, masks, flip=0):
    n, cores = lax.axis_size("dp"), lax.axis_size("tp")
    pairs = [(d * cores + c, (d ^ masks[c]) * cores + (c ^ flip)) for d in range(n) for c in range(cores)]
    return lax.ppermute(value, ("dp", "tp"), pairs)


def sibling(value):
    return lax.ppermute(value, "tp", [(0, 1), (1, 0)])


def request_table(asked, ranks, cap, width):
    count = asked.shape[1]

    def body(asked_ref, out_ref):
        hrow = jnp.broadcast_to(asked_ref[0:1, :], (count, count))
        srow = jnp.broadcast_to(asked_ref[1:2, :], (count, count))
        i, j = iota((count, count), 0), iota((count, count), 1)
        hcol = jnp.sum(jnp.where(i == j, hrow, 0), axis=1, keepdims=True)
        scol = jnp.sum(jnp.where(i == j, srow, 0), axis=1, keepdims=True)
        rank = jnp.sum(jnp.where((hrow == hcol) & (j < i), 1, 0), axis=1, keepdims=True)
        lane = hcol * cap + rank
        hit = jnp.where(iota((count, width), 1) == lane, scol + 1, 0)
        row = jnp.sum(hit, axis=0, keepdims=True)
        out_ref[...] = jnp.where(iota((ranks, width), 0) == lax.axis_index("dp"), row, 0)

    return call(body, 0, 1, [jax.ShapeDtypeStruct((ranks, width), jnp.int32)], 4)(asked)


def paired(page, page_width):
    out = []
    for b in range(0, page_width, PAIR):
        out.append(page[:, b : b + 512])
        out.append(page[:, b + 576 : b + 1088])
        out.append(jnp.concatenate([page[:, b + 512 : b + 576], page[:, b + 1088 : b + 1152]], axis=1))
    return jnp.concatenate(out, axis=1)


def prepare(queries, heads):
    tokens = queries.shape[0]

    def body(q_ref, qe_out, qo_out):
        zero = jnp.zeros((tokens, ROTARY_WIDTH), bf16)
        for h in range(heads):
            b = h * WIDTH
            nope = q_ref[:, b : b + 512]
            rope = q_ref[:, b + 512 : b + 576]
            rows = slice(h * tokens, (h + 1) * tokens)
            qe_out[rows, 0:512] = nope
            qo_out[rows, 0:512] = nope
            qe_out[rows, 512:640] = jnp.concatenate([rope, zero], axis=1)
            qo_out[rows, 512:640] = jnp.concatenate([zero, rope], axis=1)

    q_shape = jax.ShapeDtypeStruct((heads * tokens, PADDED), bf16)
    return call(body, 0, 1, [q_shape, q_shape])(queries)


def pair_pool(pool):
    def body(pool_ref, out_ref):
        out_ref[...] = paired(pool_ref[...], pool_ref.shape[1])

    return call(body, 0, 1, [jax.ShapeDtypeStruct(pool.shape, bf16)])(pool)


def stack_keys(page_ref, rows, page_width):
    pairs = page_width // PAIR
    even = jnp.concatenate([page_ref[rows, j * PAIR : j * PAIR + 512] for j in range(pairs)], axis=0)
    odd = jnp.concatenate([page_ref[rows, j * PAIR + 512 : j * PAIR + 1024] for j in range(pairs)], axis=0)
    rope = jnp.concatenate([page_ref[rows, j * PAIR + 1024 : j * PAIR + 1152] for j in range(pairs)], axis=0)
    return even, odd, rope


def dot_nt(a, b):
    return lax.dot_general(a, b, (((1,), (1,)), ((), ())), preferred_element_type=f32)


def decode(lens, pool, qe, begin, end, before=None):
    rows, heads, _ = qe.shape
    pages, page_width = pool.shape
    per_row = pages // rows
    pairs = page_width // PAIR

    def body(len_ref, pool_ref, q_ref, *refs):
        out_ref = refs[-1]
        key_rows = pairs * per_row
        s = iota((heads, key_rows), 1)
        pos = (s % per_row) * (2 * pairs) + 2 * (s // per_row)
        zero = jnp.zeros((heads, ROTARY_WIDTH), bf16)
        done = [] if before is None else [refs[0][...]]
        for g in range(begin, end):
            even, odd, rope = stack_keys(pool_ref, slice(g * per_row, (g + 1) * per_row), page_width)
            nope_q = q_ref[g, :, 0:512]
            rope_q = q_ref[g, :, 512:576]
            re = jnp.concatenate([rope_q, zero], axis=1)
            ro = jnp.concatenate([zero, rope_q], axis=1)
            se = dot_nt(nope_q, even) + dot_nt(re, rope)
            so = dot_nt(nope_q, odd) + dot_nt(ro, rope)
            se = jnp.where(pos < len_ref[g], se, masked_score)
            so = jnp.where(pos + 1 < len_ref[g], so, masked_score)
            peak = jnp.maximum(jnp.max(se, axis=1, keepdims=True), jnp.max(so, axis=1, keepdims=True))
            pe = jnp.exp2((se - peak) * exp2_scale)
            po = jnp.exp2((so - peak) * exp2_scale)
            den = jnp.sum(pe, axis=1, keepdims=True) + jnp.sum(po, axis=1, keepdims=True)
            out = jnp.dot(pe.astype(bf16), even, preferred_element_type=f32)
            out += jnp.dot(po.astype(bf16), odd, preferred_element_type=f32)
            done.append((out / den).astype(bf16))
        done = jnp.concatenate(done, axis=0)
        if before is None:
            out_ref[...] = done
            return
        i, j = iota((rows * heads, rows * heads), 0), iota((rows * heads, rows * heads), 1)
        swap = jnp.where(j == (i % rows) * heads + i // rows, 1.0, 0.0).astype(bf16)
        done = jnp.dot(swap, done, preferred_element_type=f32)
        for h in range(heads):
            out_ref[:, h * LATENT_WIDTH : (h + 1) * LATENT_WIDTH] = done[h * rows : (h + 1) * rows, :].astype(bf16)

    if before is None:
        out = jax.ShapeDtypeStruct(((end - begin) * heads, LATENT_WIDTH), bf16)
        return call(body, 1, 2, [out])(lens, pool, qe)
    out = jax.ShapeDtypeStruct((rows, heads * LATENT_WIDTH), bf16)
    return call(body, 1, 3, [out])(lens, pool, qe, before)


def gather_pages(table, pool, suffix, streams, cap):
    ranks, width = table.shape
    pages, page_width = pool.shape
    block = TEAM * cap
    total = sum(half for _, half in streams)

    def body(table_ref, pool_ref, *outs):
        if suffix is not None:
            suffix_ref, outs = outs[0], outs[1:]
        me, core = lax.axis_index("dp"), lax.axis_index("tp")
        team = me // TEAM
        tab = table_ref[...].astype(f32).astype(bf16)

        def position(shape):
            n = iota(shape, 0)
            g = jnp.zeros(shape, jnp.int32)
            base = jnp.zeros(shape, jnp.int32)
            at = 0
            for first, half in streams:
                inside = (n >= at) & (n < at + half)
                g = jnp.where(inside, n - at + (core if first == 0 else 1 - core) * half, g)
                base = jnp.where(inside, first, base)
                at += half
            return base, g

        base, g = position((total, ranks))
        source = (team ^ (base + g // block)) * TEAM + (g % block) // cap
        pick = jnp.where(iota((total, ranks), 1) == source, 1.0, 0.0).astype(bf16)
        spread = jnp.dot(pick, tab, preferred_element_type=f32)
        _, g = position((total, width))
        mine = iota((total, width), 1) == me * cap + g % cap
        slot = jnp.sum(jnp.where(mine, spread, 0.0), axis=1, keepdims=True)
        hot = jnp.where(iota((total, pages), 1) + 1 == slot.astype(jnp.int32), 1.0, 0.0).astype(bf16)
        rows = jnp.dot(hot, pool_ref[...], preferred_element_type=f32).astype(bf16)
        at = 0
        for n, (_, half) in enumerate(streams):
            outs[n][:, 0:page_width] = rows[at : at + half]
            at += half
            if suffix is not None and n == 0:
                left = suffix_ref[:, 0:SUFFIX_LANES]
                right = suffix_ref[:, SUFFIX_LANES : 2 * SUFFIX_LANES]
                if half > left.shape[0]:
                    outs[n][:, page_width:] = jnp.zeros((half, SUFFIX_LANES), bf16)
                outs[n][0 : left.shape[0], page_width:] = jnp.where(core == 0, left, right)

    outs = [
        jax.ShapeDtypeStruct((half, page_width + (SUFFIX_LANES if n == 0 and suffix is not None else 0)), bf16)
        for n, (_, half) in enumerate(streams)
    ]
    given = [table, pool] + ([] if suffix is None else [suffix])
    out = call(body, 0, len(given), outs)(*given)
    return out if len(outs) > 1 else (out,)


def key_masks(table, streams, cap, orders, tokens):
    ranks, width = table.shape
    block = TEAM * cap

    def body(table_ref, *outs):
        me, core = lax.axis_index("dp"), lax.axis_index("tp")
        team, member = me // TEAM, me % TEAM
        tab = table_ref[...].astype(f32).astype(bf16)
        for n, (base, half) in enumerate(streams):
            total = TEAM * half
            for side in range(2):
                p = iota((width, total), 1)
                b, i = p // half, p % half
                owner = (core + side + b // 4) % 2
                away = jnp.zeros((width, total), jnp.int32)
                for k in range(3):
                    step = jnp.where(owner == 0, orders[n][0][k], orders[n][1][k])
                    away += ((b // (1 << k)) % 2) * step
                g = owner * half + i
                holder = (team ^ (base + g // block)) * TEAM + (member ^ away)
                sel = jnp.where(iota((width, total), 0) == holder * cap + g % cap, 1.0, 0.0).astype(bf16)
                q = iota((ranks, total), 1)
                asker = team * TEAM + (((core + side + q // (4 * half)) % 2 * half + q % half) % block) // cap
                found = jnp.dot(tab, sel, preferred_element_type=f32)
                found = jnp.sum(jnp.where(iota((ranks, total), 0) == asker, found, 0.0), axis=0, keepdims=True)
                found = jnp.where(found > 0.0, 0.0, masked_score)
                for k in range(4):
                    wide = []
                    for at in range(k * 2 * half, (k + 1) * 2 * half, min(2 * half, CHUNK // 2)):
                        wide += [found[:, at : at + min(2 * half, CHUNK // 2)]] * tokens
                    outs[n][side * 4 + k : side * 4 + k + 1, :] = jnp.concatenate(wide, axis=1)

    outs = [jax.ShapeDtypeStruct((8, 2 * half * tokens), f32) for _, half in streams]
    out = call(body, 0, 1, outs)(table)
    return out if len(outs) > 1 else (out,)


def softmax_step(s_ref, p_ref, width, bias, causal, old_state, new_state, values, row_block):
    m_old, l_old, acc_old = old_state
    m_ref, l_ref, acc_ref = new_state
    total = s_ref.shape[0]
    for r in range(0, total, row_block):
        rows = slice(r, r + row_block)
        if causal is None:
            scores = s_ref[rows, 0:width] + bias
        else:
            plain = bias.shape[1]
            scores = jnp.concatenate([s_ref[rows, 0:plain] + bias, s_ref[rows, plain:width] + causal(r, row_block)], axis=1)
        peak = jnp.max(scores, axis=1, keepdims=True)
        if m_old is None:
            peak = jnp.broadcast_to(peak, (row_block, LANES))
        else:
            peak = jnp.maximum(m_old[rows, :], peak)
        powers = jnp.exp2((scores - jnp.concatenate([peak] * (width // LANES), axis=1)) * exp2_scale)
        added = jnp.sum(powers, axis=1, keepdims=True)
        if m_old is None:
            l_ref[rows, :] = jnp.broadcast_to(added, (row_block, LANES))
        else:
            factor = jnp.exp2((m_old[rows, :] - peak) * exp2_scale)
            l_ref[rows, :] = l_old[rows, :] * factor + added
            acc_ref[rows, :] = acc_old[rows, :] * jnp.concatenate([factor] * (LATENT_WIDTH // LANES), axis=1)
        m_ref[rows, :] = peak
        p_ref[rows, 0:width] = powers.astype(bf16)
    add = jnp.dot(p_ref[:, 0:width], values, preferred_element_type=f32)
    if m_old is None:
        acc_ref[...] = add
    else:
        acc_ref[...] += add


def state_shapes(total):
    stat = jax.ShapeDtypeStruct((total, LANES), f32)
    return [stat, stat, jax.ShapeDtypeStruct((total, LATENT_WIDTH), f32)]


def collect_suffix(key_ref, came, orders, page_width, share):
    core, member = lax.axis_index("tp"), lax.axis_index("dp") % TEAM
    half = came[0].shape[0] // 2
    for b in range(TEAM):
        rows = slice((b % 2) * half, (b % 2) * half + share)
        mine, theirs = came[b // 2][rows, page_width:], came[4 + b // 2][rows, page_width:]
        for side in range(2):
            piece = jnp.where(core == side ^ (b // 4), mine, theirs)
            source = member ^ sum(orders[side][k] for k in range(3) if (b >> k) & 1)
            at = pl.ds(pl.multiple_of(source * share, share), share)
            if side == 0:
                key_ref[at, 0:SUFFIX_LANES] = piece
            else:
                key_ref[at, SUFFIX_LANES:PADDED] = piece[:, 0 : PADDED - SUFFIX_LANES]


def attend(state, qe, qo, parts, page_width, row_block, suffix_len, tokens, suffix=None, last=None):
    n = len(parts)
    total = qe.shape[0]
    first = state is None
    per = page_width // WIDTH
    pieces = []
    for k, (page, _, _) in enumerate(parts):
        step = min(page.shape[0], CHUNK // 2)
        pieces += [(k, at, step) for at in range(0, page.shape[0], step)]
    groups, size = [[]], 0
    for piece in pieces:
        if size + piece[2] > CHUNK:
            groups.append([])
            size = 0
        groups[-1].append(piece)
        size += piece[2]
    widest = max(sum(p[2] for p in g) for g in groups) * per + (tokens if suffix else 0)
    n_came = 8 if suffix else 0

    def body(len_ref, qe_ref, qo_ref, *refs):
        page_refs, bias_refs, refs = refs[:n], refs[n : 2 * n], refs[2 * n :]
        came, refs = refs[:n_came], refs[n_came:]
        old = (None, None, None)
        if not first:
            old, refs = tuple(refs[:3]), refs[3:]
        if last:
            out_ref, refs = refs[0], refs[1:]
        new = tuple(refs[:3])
        s_ref, p_ref = refs[3:5]
        length = len_ref[lax.axis_index("dp") // TEAM]
        for number, group in enumerate(groups):
            evens, odds, ropes, even_bias, odd_bias = [], [], [], [], []
            for k, at, step in group:
                even, odd, rope = stack_keys(page_refs[k], slice(at, at + step), page_width)
                evens.append(even)
                odds.append(odd)
                ropes.append(rope)
                row, half_keys = parts[k][2], step * per // 2
                even_bias.append(bias_refs[k][row : row + 1, at * per : at * per + half_keys])
                odd_bias.append(bias_refs[k][row : row + 1, at * per + half_keys : at * per + 2 * half_keys])
            rope = jnp.concatenate(ropes, axis=0)
            even, odd = jnp.concatenate(evens, axis=0), jnp.concatenate(odds, axis=0)
            width = even.shape[0]
            s_ref[:, 0:width] = dot_nt(qe_ref[...], jnp.concatenate([even, rope], axis=1))
            s_ref[:, width : 2 * width] = dot_nt(qo_ref[...], jnp.concatenate([odd, rope], axis=1))
            width *= 2
            values, causal = [even, odd], None
            if suffix and number == len(groups) - 1:
                key_ref = refs[5]
                collect_suffix(key_ref, came, suffix[1], page_width, tokens // TEAM)
                s_ref[:, width : width + tokens] = dot_nt(qe_ref[...], key_ref[...])
                width += tokens
                values.append(key_ref[:, 0:LATENT_WIDTH])

                def causal(r, count):
                    u = iota((count, tokens), 1)
                    t = (iota((count, tokens), 0) + r) % tokens
                    return jnp.where((u <= t) & (u < length), 0.0, masked_score)

            bias = jnp.concatenate(even_bias + odd_bias, axis=1)
            softmax_step(s_ref, p_ref, width, bias, causal, old, new, jnp.concatenate(values, axis=0), row_block)
            old = new
        if last:
            _, l_ref, acc_ref = new
            live = iota((tokens, LATENT_WIDTH), 0) < length
            for h in range(last):
                rows = slice(h * tokens, (h + 1) * tokens)
                share = 1.0 / l_ref[rows, :]
                out = acc_ref[rows, :] * jnp.concatenate([share] * (LATENT_WIDTH // LANES), axis=1)
                out_ref[:, h * LATENT_WIDTH : (h + 1) * LATENT_WIDTH] = jnp.where(live, out, 0.0).astype(bf16)

    pages = [p for p, _, _ in parts]
    biases = [b for _, b, _ in parts]
    came = list(suffix[0]) if suffix else []
    carried = [] if first else list(state)
    n_in = 2 + 2 * n + len(came) + len(carried)
    scratch = [pltpu.VMEM((total, widest), f32), pltpu.VMEM((total, widest), bf16)]
    if suffix:
        scratch.append(pltpu.VMEM((tokens, PADDED), bf16))
    mib = 9 + (sum(p.size * 2 for p in pages + came) >> 20)
    outs = state_shapes(total)
    if last:
        scratch = [pltpu.VMEM(x.shape, f32) for x in outs] + scratch
        outs = [jax.ShapeDtypeStruct((tokens, last * LATENT_WIDTH), bf16)]
    return call(body, 1, n_in, outs, mib, scratch_shapes=scratch)(suffix_len, qe, qo, *pages, *biases, *came, *carried)


def program(pool, page_holder, page_slot, suffix_latent_rows, prefill_queries, suffix_len, decode_queries, decode_len):
    ranks = lax.axis_size("dp")
    teams = ranks // TEAM
    pull = page_holder.shape[0]
    cap = (pull + ranks - 1) // ranks
    width = -(-ranks * cap // LANES) * LANES
    page_width = pool.shape[1]
    tokens = prefill_queries.shape[1]
    heads = prefill_queries.shape[2] // WIDTH
    share = suffix_latent_rows.shape[1] // WIDTH

    table = request_table(jnp.stack([page_holder, page_slot]), ranks, cap, width)
    block = TEAM * cap
    split = block % 32 == 0
    if split:
        streams = [(j, block // 2) for j in range(teams)]
    else:
        streams = [(0, teams * block // 2)]
    suffix = jnp.pad(suffix_latent_rows.reshape(share, WIDTH), ((0, 0), (0, 2 * SUFFIX_LANES - WIDTH)))
    pool = pair_pool(pool)
    sent = []
    step = 1
    while step < ranks:
        table = table + xperm(table, (step, step), 1)
        step *= 2
        if step == TEAM and split:
            sent += gather_pages(table, pool, suffix, streams[:1], cap)
    if split:
        sent += gather_pages(table, pool, None, streams[1:], cap)
    else:
        sent += gather_pages(table, pool, suffix, streams, cap)
    qe, qo = prepare(prefill_queries[0], heads)
    dq = decode_queries.reshape(decode_queries.shape[0], -1, WIDTH)
    middle = dq.shape[0] // 2
    some = decode(decode_len, pool, dq, 0, middle)
    decode_part = decode(decode_len, pool, dq, middle, dq.shape[0], some)

    orders = [((4, 1, 2), (4, 2, 1)), ((1, 2, 4), (2, 4, 1))]
    orders = [orders[n % 2] for n in range(len(streams))]
    masks_of = key_masks(table, streams, cap, orders, page_width // WIDTH)

    came = []
    for n, (base, half) in enumerate(streams):
        rows = sent[n]
        unit = min(block, half)
        pieces = []
        for at in range(0, half, unit):
            masks = tuple(TEAM * (base + (c * half + at) // block) for c in range(2))
            piece = rows[at : at + unit, :page_width] if half > unit else rows
            pieces.append(xperm(piece, masks, int(split)) if any(masks) else piece)
        if half > unit:
            rows = jnp.concatenate([jnp.concatenate(pieces, axis=0), rows[:, page_width:]], axis=1)
        else:
            rows = pieces[0]
        masks = list(zip(*orders[n]))
        got = xperm(rows, masks[0])
        both = jnp.concatenate([rows, got], axis=0)
        second = xperm(both, masks[1])
        third = xperm(both, masks[2], 1)
        fourth = xperm(second, masks[2], 1)
        own = [both, second, third, fourth]
        other = []
        for piece in own:
            other.append(sibling(piece))
        came.append((own, other))

    row_block = 128
    pieces = []
    for n in range(len(streams)):
        own, other = came[n]
        pieces.append([[(own[k], masks_of[n], k), (other[k], masks_of[n], 4 + k)] for k in range(4)])
    if len(streams) > 1:
        plan = [("att0a", pieces[0][0]), ("att0f", pieces[0][1]), ("att1a", pieces[1][0])]
        plan += [("att0e", pieces[0][2]), ("att0b", pieces[0][3])]
        for n in range(1, len(streams)):
            if n > 1:
                plan.append((f"att{n}a", pieces[n][0]))
            plan += [(f"att{n}b", pieces[n][1]), (f"att{n}d", pieces[n][2]), (f"att{n}c", pieces[n][3])]
    else:
        plan = [("att0a", pieces[0][0] + pieces[0][1]), ("att0b", pieces[0][2]), ("att0c", pieces[0][3])]
    tail = "att0b" if len(streams) > 1 else plan[-1][0]
    state = None
    for n, (name, group) in enumerate(plan):
        suffix = (came[0][0] + came[0][1], orders[0]) if name == tail else None
        last = heads if n == len(plan) - 1 else None
        state = attend(state, qe, qo, group, page_width, row_block, suffix_len, tokens, suffix, last)
    return (state[None], decode_part)


def solution(mesh):
    placed = (
        P(("groups", "dp"), None),
        P(("groups", "dp")),
        P(("groups", "dp")),
        P(("groups", "dp"), None),
        P(("groups", "dp"), None, "tp"),
        P("groups"),
        P(("groups", "dp"), "tp"),
        P(("groups", "dp")),
    )
    return jax.shard_map(
        program,
        mesh=mesh,
        in_specs=placed,
        out_specs=(P(("groups", "dp"), None, "tp"), P(("groups", "dp"), "tp")),
        check_vma=False,
    )
```
